32 devices in a mesh: var: 16 (over z, y, core), samp: 2 (over x).
Axes of the slice: x: 2, y: 2, z: 4, core: 2. Of those that a mesh axis runs over, the one named last changes fastest.
Arguments:
- genotypes: bfloat16 [4096, 12288], P('samp', 'var'), may hold values from -6 to 6
- marginal: float32 [12288, 1024], P('var', 'samp'), may hold values from -6 to 6
- start_effects: float32 [12288, 1024], P('var', 'samp'), may hold values from -5 to 5
- thresholds: float32 [1024], P('samp'), may hold values from 0.02 to 0.5
Outputs:
- shrunk_effects: float32 [12288, 1024], P('var', 'samp')
The draws below stay inside these ranges and needn't reach their ends.
All inputs are finite; a program needn't handle non-finite values.
Results may differ from the reference program's by a relative error of at most 0.0003.
Values may be sent and summed in bfloat16 or wider, within the bound.
A program may use at most 64 MiB of HBM per device.

```python
import math
import jax
import jax.numpy as jnp
from jax import lax

TILE = 256
TRAITS = 1024
SWEEPS = 2
VARIANTS = 12288
NSAMP = 4096


def level_of(stream_key, extent, shards, least, top_value):
    def one(position, parts):
        heights = jax.random.uniform(jax.random.fold_in(jax.random.fold_in(stream_key, 6), position), (parts,), jnp.float32, least / len(shards), top_value / len(shards))
        return jnp.repeat(jnp.exp(heights), extent[position] // parts).reshape((-1,) + (1,) * (len(extent) - position - 1))

    factor_of = one(*shards[0])
    for cut in shards[1:]:
        factor_of = factor_of * one(*cut)
    return factor_of


def bell_draw(key, extent, width, most, pieces=(), held_as=jnp.bfloat16):
    loudness = level_of(key, extent, pieces, -0.22, 0.18) if pieces else 1.0
    entries = jax.random.normal(key, extent, jnp.float32) * width * loudness
    return jnp.minimum(jnp.maximum(entries, -most), most).astype(held_as)


def setup_inputs(seed: int = 0) -> dict:
    keys = jax.random.split(jax.random.key(seed), 5)
    return {
        "genotypes": bell_draw(keys[0], (NSAMP, VARIANTS), 1.0, 6.0, ((0, 2), (1, 16))),
        "marginal": bell_draw(keys[1], (VARIANTS, TRAITS), 1.0, 6.0, ((0, 16), (1, 2)), jnp.float32),
        "start_effects": bell_draw(keys[2], (VARIANTS, TRAITS), 0.7, 5.0, ((0, 16), (1, 2)), jnp.float32),
        "thresholds": jnp.clip(jnp.exp(math.log(0.5) - 3.218876 * jax.random.uniform(keys[3], (TRAITS,), jnp.float32) ** level_of(keys[3], (TRAITS,), ((0, 2),), -0.2, 0.2)), 0.02, 0.5),
    }


shrinkage = 0.2


def reference(genotypes, marginal, start_effects, thresholds):
    tile_count = VARIANTS // TILE

    def gram_tile(index):
        left_tile = lax.dynamic_slice_in_dim(genotypes, index * TILE, TILE, 1).astype(jnp.float32)
        right_start = jnp.minimum(index + 1, tile_count - 1).astype(jnp.int32) * TILE
        right_tile = lax.dynamic_slice_in_dim(genotypes, right_start, TILE, 1).astype(jnp.float32)
        paired = jnp.concatenate([left_tile, right_tile], axis=1)
        return lax.dot_general(left_tile, paired, (((0,), (0,)), ((), ())), preferred_element_type=jnp.float32)

    products = lax.map(gram_tile, jnp.arange(tile_count, dtype=jnp.int32)) / NSAMP
    diag_tiles = products[:, :, :TILE]
    keep_upper = (jnp.arange(tile_count) < tile_count - 1).astype(jnp.float32)
    upper_tiles = products[:, :, TILE:] * keep_upper[:, None, None]
    lower_tiles = jnp.concatenate([jnp.zeros((1, TILE, TILE), jnp.float32), jnp.transpose(upper_tiles[:-1], (0, 2, 1))], axis=0)
    ld_diagonal = jnp.diagonal(diag_tiles, axis1=1, axis2=2).reshape(VARIANTS)
    divisor = (1.0 - shrinkage) * ld_diagonal + shrinkage
    limit_rows = thresholds[None, :]
    effects = start_effects
    empty = jnp.zeros((1, TILE, TRAITS), jnp.float32)
    high = lax.Precision.HIGHEST
    for sweep_index in range(SWEEPS):
        blocks = effects.reshape(tile_count, TILE, TRAITS)
        earlier = jnp.concatenate([empty, blocks[:-1]], axis=0)
        following = jnp.concatenate([blocks[1:], empty], axis=0)
        combined = jnp.einsum("tij,tjk->tik", diag_tiles, blocks, precision=high)
        combined = combined + jnp.einsum("tij,tjk->tik", lower_tiles, earlier, precision=high)
        combined = combined + jnp.einsum("tij,tjk->tik", upper_tiles, following, precision=high)
        combined = combined.reshape(VARIANTS, TRAITS)
        cross_term = (1.0 - shrinkage) * (combined - ld_diagonal[:, None] * effects)
        adjusted = marginal - cross_term
        effects = (adjusted - jnp.clip(adjusted, -limit_rows, limit_rows)) / divisor[:, None]
    return effects
```

```python
import functools

import jax
import jax.numpy as jnp
from jax import lax
from jax.experimental import pallas as pl
from jax.experimental.pallas import tpu as pltpu
from jax.sharding import PartitionSpec as P

TILE = 256
HALF = TILE // 2
SWEEPS = 2
CHUNKS = 4
BACK_FIRST = 2
BACK_LAST = 4
TINY = 2.0**-126
VMEM_BYTES = 40 * 1024 * 1024
LD_SCALE = 1024.0

shrinkage = 0.2
MESH = pl.DeviceIdType.MESH
F32 = jnp.float32
BF16 = jnp.bfloat16


def encode(value):
    square = value * value
    fourth = square * square
    eighth = fourth * fourth
    return jnp.where(value < 0, -eighth, eighth).astype(BF16)


def decode(code):
    code = code.astype(F32)
    size = jnp.abs(code)
    fourth_root = lax.rsqrt(lax.rsqrt(jnp.maximum(size, TINY)))
    root = jnp.where(size < TINY, 0.0, fourth_root * lax.rsqrt(fourth_root))
    return jnp.where(code < 0, -root, root)


def encode_wide(value):
    square = value * value
    fourth = square * square
    return jnp.where(value < 0, -fourth, fourth).astype(BF16)


def decode_wide(code):
    code = code.astype(F32)
    size = jnp.abs(code)
    root = jnp.where(size < TINY, 0.0, lax.rsqrt(lax.rsqrt(jnp.maximum(size, TINY))))
    return jnp.where(code < 0, -root, root)


def split(value):
    high = value.astype(BF16)
    return high, (value - high.astype(F32)).astype(BF16)


def iota_pair(size):
    row = lax.broadcasted_iota(jnp.int32, (size, size), 0)
    col = lax.broadcasted_iota(jnp.int32, (size, size), 1)
    return row, col


def pack_symmetric(tile):
    row, col = iota_pair(HALF)
    mixed = jnp.where(row < col, tile[:HALF, :HALF], tile[HALF:, HALF:])
    return jnp.concatenate([mixed, tile[:HALF, HALF:]], axis=1)


def unpack_symmetric(packed):
    row, col = iota_pair(HALF)
    mixed, corner = packed[:, :HALF], packed[:, HALF:]
    upper = jnp.where(row < col, mixed, 0.0)
    lower = jnp.where(row > col, mixed, 0.0)
    first = jnp.concatenate([upper + upper.T, corner], axis=1)
    second = jnp.concatenate([corner.T, lower + lower.T], axis=1)
    return jnp.concatenate([first, second], axis=0)


def gram(left, right):
    return lax.dot_general(left, right, (((0,), (0,)), ((), ())), preferred_element_type=F32)


def kernel(
    tiles, var_size, samp_size, inv_total,
    geno_hbm, marg_hbm, start_hbm, limit_hbm, out,
    geno, halo, marg, start, limit_row, own, code, got, diag, diag_got,
    band_hi, band_lo, eff_hi, eff_lo, cross_hi, cross_lo, first_term,
    early_code, early_got, tail_diag, tail_got, back_code, back_got,
    load_sem, geno_send, geno_recv, part_send, part_recv,
    early_send, early_recv, back_send, back_recv,
):
    var = lax.axis_index("var")
    samp = lax.axis_index("samp")
    has_prev = var > 0
    has_next = var < var_size - 1
    prev, following = var - 1, var + 1
    peers = [lax.rem(samp + k, samp_size) for k in range(1, samp_size)]
    last = tiles - 1
    tail = slice(last * TILE, tiles * TILE)

    step = HALF + TILE
    cross_at = tiles * step - TILE
    halves = range(2)
    diag_message = tiles + 2

    loads = []
    for t in range(tiles):
        cols = pl.ds(t * TILE, TILE)
        loads.append(pltpu.make_async_copy(geno_hbm.at[:, cols], geno.at[:, cols], load_sem.at[t]))
    loads.append(pltpu.make_async_copy(start_hbm, start, load_sem.at[tiles]))
    loads.append(pltpu.make_async_copy(marg_hbm, marg, load_sem.at[tiles + 1]))
    loads.append(pltpu.make_async_copy(limit_hbm, limit_row, load_sem.at[tiles + 2]))
    for copy in loads:
        copy.start()

    barrier = pltpu.get_barrier_semaphore()

    @pl.when(has_prev)
    def _():
        pl.semaphore_signal(barrier, inc=1, device_id={"var": prev}, device_id_type=MESH)

    @pl.when(has_next)
    def _():
        pl.semaphore_signal(barrier, inc=1, device_id={"var": following}, device_id_type=MESH)

    for peer in peers:
        pl.semaphore_signal(barrier, inc=1, device_id={"samp": peer}, device_id_type=MESH)
    pl.semaphore_wait(
        barrier, len(peers) + has_prev.astype(jnp.int32) + has_next.astype(jnp.int32)
    )

    depth = geno.shape[0] // CHUNKS
    chunks = [(half, chunk) for half in halves for chunk in range(CHUNKS)]

    def geno_copy(half, chunk):
        rows = pl.ds(chunk * depth, depth)
        return pltpu.make_async_remote_copy(
            src_ref=geno_hbm.at[rows, pl.ds(last * TILE + half * HALF, HALF)],
            dst_ref=halo.at[rows, pl.ds(half * HALF, HALF)],
            send_sem=geno_send.at[half, chunk], recv_sem=geno_recv.at[half, chunk],
            device_id={"var": following}, device_id_type=MESH,
        )

    @pl.when(has_next)
    def _():
        for half, chunk in chunks:
            geno_copy(half, chunk).start()

    def part_copy(k, message):
        if message == diag_message:
            src, dst = diag, diag_got.at[k]
        else:
            if message < tiles:
                rows = pl.ds(message * step, HALF if message == last else step)
            else:
                rows = pl.ds(cross_at + (message - tiles) * HALF, HALF)
            src, dst = code.at[rows], got.at[k, rows]
        return pltpu.make_async_remote_copy(
            src_ref=src, dst_ref=dst,
            send_sem=part_send.at[k, message], recv_sem=part_recv.at[k, message],
            device_id={"samp": peers[k]}, device_id_type=MESH,
        )

    def send_part(message):
        for k in range(len(peers)):
            part_copy(k, message).start()

    def take_part(message):
        for k in range(len(peers)):
            part_copy(k, message).wait_recv()

    diag[...] = jnp.zeros_like(diag)
    row, col = iota_pair(TILE)
    on_diagonal = row == col

    for t in range(tiles):
        if t == 0:
            loads[0].wait()
        if t + 1 < tiles:
            loads[t + 1].wait()
        reach = min(t + 2, tiles) * TILE
        product = gram(geno[:, t * TILE : (t + 1) * TILE], geno[:, t * TILE : reach])
        product = product * (inv_total * LD_SCALE)
        block = product[:, :TILE]
        diag[pl.ds(t, 1), :] = jnp.sum(jnp.where(on_diagonal, block, 0.0), axis=0, keepdims=True)
        begin = t * step
        packed = pack_symmetric(block)
        own[begin : begin + HALF] = packed
        code[begin : begin + HALF] = encode(packed)
        if t + 1 < tiles:
            beside = product[:, TILE:]
            own[begin + HALF : begin + step] = beside
            code[begin + HALF : begin + step] = encode(beside)
        if t == last:
            send_part(diag_message)
        send_part(t)

    for copy in loads[tiles:]:
        copy.wait()

    def place(sweep, slot, value, first=0):
        begin = slot * TILE + first
        high, low = split(value)
        eff_hi[sweep, begin : begin + value.shape[0]] = high
        eff_lo[sweep, begin : begin + value.shape[0]] = low

    early = [(early_code.at[k], early_got.at[k]) for k in range(2)] + [(tail_diag, tail_got)]

    def early_copy(k):
        src, dst = early[k]
        return pltpu.make_async_remote_copy(
            src_ref=src, dst_ref=dst, send_sem=early_send.at[k], recv_sem=early_recv.at[k],
            device_id={"var": following}, device_id_type=MESH,
        )

    def send_early(k):
        @pl.when(has_next)
        def _():
            early_copy(k).start()

    early_code[0] = encode(start[tail])
    send_early(0)
    for t in range(tiles):
        place(0, t + 1, start[t * TILE : (t + 1) * TILE])

    def summed(begin, size):
        value = own[begin : begin + size]
        for k in range(len(peers)):
            value = value + decode(got[k, begin : begin + size])
        return value

    def put(tile, slot, value, first=0):
        high, low = split(value)
        begin = slot * TILE + first
        band_hi[tile, :, begin : begin + value.shape[1]] = high
        band_lo[tile, :, begin : begin + value.shape[1]] = low

    dot = functools.partial(jnp.dot, preferred_element_type=F32)

    def applied(sweep, tile, first, count):
        across = slice(first * TILE, (first + count) * TILE)
        rows = slice((tile + first) * TILE, (tile + first + count) * TILE)
        high, low = band_hi[tile, :, across], band_lo[tile, :, across]
        near, rest = eff_hi[sweep, rows], eff_lo[sweep, rows]
        return dot(high, near) + (dot(high, rest) + dot(low, near))

    def add_tile(t):
        take_part(t)
        begin = t * step
        put(t, 1, unpack_symmetric(summed(begin, HALF)) * (1.0 / LD_SCALE))
        if t + 1 < tiles:
            beside = summed(begin + HALF, TILE) * (1.0 / LD_SCALE)
            put(t, 2, beside)
            put(t + 1, 0, beside.T)

    def cross_step(now):
        @pl.when(jnp.logical_and(has_prev, now))
        def _():
            for half in halves:
                crossing = jnp.zeros((HALF, TILE), F32)
                for chunk in range(CHUNKS):
                    rows = slice(chunk * depth, (chunk + 1) * depth)
                    geno_copy(half, chunk).wait_recv()
                    crossing = crossing + gram(
                        halo[rows, half * HALF : (half + 1) * HALF], geno[rows, :TILE]
                    )
                crossing = crossing * (inv_total * LD_SCALE)
                begin = cross_at + half * HALF
                own[begin : begin + HALF] = crossing
                code[begin : begin + HALF] = encode(crossing)
                send_part(tiles + half)

    nearby = lax.rem(var, 2) == 1
    cross_step(nearby)
    for t in range(tiles):
        add_tile(t)
    take_part(diag_message)

    def keep_of(whole):
        column = jnp.sum(jnp.where(on_diagonal, whole, 0.0), axis=1, keepdims=True) * (1.0 / LD_SCALE)
        return 1.0 / ((1.0 - shrinkage) * column + shrinkage)

    keep = []
    for t in range(tiles):
        whole = diag[pl.ds(t, 1), :]
        for k in range(len(peers)):
            whole = whole + diag_got[k, pl.ds(t, 1), :]
        keep.append(keep_of(whole))
        if t == last:
            tail_diag[...] = jnp.broadcast_to(whole, tail_diag.shape)
    limit = limit_row[...]

    def adjust(tile, combined, rows=slice(0, TILE)):
        shift = slice(tile * TILE + rows.start, tile * TILE + rows.stop)
        return (marg[shift] - (1.0 - shrinkage) * combined) * keep[tile][rows]

    def soften(value, scale):
        bound = limit * scale
        return value - jnp.clip(value, -bound, bound)

    def finish(tile, combined, rows=slice(0, TILE)):
        return soften(adjust(tile, combined, rows), keep[tile][rows])

    near_last = applied(0, last, 0, 2)
    early_code[1] = encode(adjust(last, near_last))
    send_early(2)
    send_early(1)
    near_first = applied(0, 0, 1, 2)
    for t in range(1, last):
        place(1, t + 1, finish(t, applied(0, t, 0, 3)))

    cross_step(jnp.logical_not(nearby))

    sizes = (BACK_FIRST, BACK_LAST)
    places = [(sweep, piece) for sweep in range(SWEEPS) for piece in range(sizes[sweep])]

    def piece_rows(sweep, piece):
        size = TILE // sizes[sweep]
        return slice(piece * size, (piece + 1) * size)

    def back_copy(sweep, piece):
        rows = piece_rows(sweep, piece)
        return pltpu.make_async_remote_copy(
            src_ref=back_code.at[sweep, pl.ds(rows.start, rows.stop - rows.start)],
            dst_ref=back_got.at[sweep, pl.ds(rows.start, rows.stop - rows.start)],
            send_sem=back_send.at[sweep, piece], recv_sem=back_recv.at[sweep, piece],
            device_id={"var": prev}, device_id_type=MESH,
        )

    def across(sweep, rows):
        near, rest = eff_hi[sweep, TILE : 2 * TILE], eff_lo[sweep, TILE : 2 * TILE]
        high, low = cross_hi[rows], cross_lo[rows]
        return dot(high, near) + (dot(high, rest) + dot(low, near))

    @pl.when(has_prev)
    def _():
        for half in halves:
            rows = piece_rows(0, half)
            take_part(tiles + half)
            crossing = summed(cross_at + half * HALF, HALF) * (1.0 / LD_SCALE)
            cross_hi[rows], cross_lo[rows] = split(crossing)
            term = across(0, rows)
            first_term[rows] = term
            back_code[0, rows] = encode(term)
            back_copy(0, half).start()
            put(0, 0, crossing.T, half * HALF)
        early_copy(0).wait_recv()
        place(0, 0, decode(early_got[0]))

    @pl.when(jnp.logical_not(has_prev))
    def _():
        put(0, 0, jnp.zeros((TILE, TILE), F32))
        for sweep in range(SWEEPS):
            place(sweep, 0, jnp.zeros((TILE, limit.shape[1]), F32))

    place(1, 1, finish(0, near_first + applied(0, 0, 0, 1)))

    @pl.when(has_prev)
    def _():
        for piece in range(BACK_LAST):
            rows = piece_rows(1, piece)
            back_code[1, rows] = encode_wide(across(1, rows))
            back_copy(1, piece).start()
        early_copy(2).wait_recv()
        early_copy(1).wait_recv()
        scale = keep_of(tail_got[pl.ds(0, 1), :])
        value = decode(early_got[1]) - (1.0 - shrinkage) * (first_term[...] * scale)
        place(1, 0, soften(value, scale))

    for t in range(last - 1):
        out[t * TILE : (t + 1) * TILE] = finish(t, applied(1, t, 0, 3))
    inner = applied(1, last - 1, 0, 2)
    edge = applied(1, last, 0, 1)

    @pl.when(jnp.logical_not(has_next))
    def _():
        back_got[...] = jnp.zeros_like(back_got)

    for piece in range(BACK_FIRST):
        rows = piece_rows(0, piece)

        @pl.when(has_next)
        def _():
            back_copy(0, piece).wait_recv()

        place(1, tiles, finish(last, near_last[rows] + decode(back_got[0, rows]), rows), rows.start)

    out[(last - 1) * TILE : last * TILE] = finish(last - 1, inner + applied(1, last - 1, 2, 1))
    edge = edge + applied(1, last, 1, 1)
    for piece in range(BACK_LAST):
        rows = piece_rows(1, piece)

        @pl.when(has_next)
        def _():
            back_copy(1, piece).wait_recv()

        combined = edge[rows] + decode_wide(back_got[1, rows])
        out[last * TILE + rows.start : last * TILE + rows.stop] = finish(last, combined, rows)

    for k in range(len(peers)):
        for message in list(range(tiles)) + [diag_message]:
            part_copy(k, message).wait_send()

    @pl.when(has_prev)
    def _():
        for k in range(len(peers)):
            for half in halves:
                part_copy(k, tiles + half).wait_send()
        for sweep, piece in places:
            back_copy(sweep, piece).wait_send()

    @pl.when(has_next)
    def _():
        for half, chunk in chunks:
            geno_copy(half, chunk).wait_send()
        for k in range(len(early)):
            early_copy(k).wait_send()


def local(genotypes, marginal, start_effects, thresholds):
    samples, variants = genotypes.shape
    traits = marginal.shape[1]
    tiles = variants // TILE
    var_size, samp_size = lax.axis_size("var"), lax.axis_size("samp")
    others = samp_size - 1
    rows = tiles * (HALF + TILE)
    dma = pltpu.SemaphoreType.DMA
    body = functools.partial(
        kernel, tiles, var_size, samp_size, 1.0 / (samples * samp_size)
    )
    return pl.pallas_call(
        body,
        out_shape=jax.ShapeDtypeStruct((variants, traits), F32),
        in_specs=[pl.BlockSpec(memory_space=pltpu.HBM)] * 4,
        out_specs=pl.BlockSpec(memory_space=pltpu.VMEM),
        scratch_shapes=[
            pltpu.VMEM((samples, variants), BF16),
            pltpu.VMEM((samples, TILE), BF16),
            pltpu.VMEM((variants, traits), F32),
            pltpu.VMEM((variants, traits), F32),
            pltpu.VMEM((1, traits), F32),
            pltpu.VMEM((rows, TILE), F32),
            pltpu.VMEM((rows, TILE), BF16),
            pltpu.VMEM((others, rows, TILE), BF16),
            pltpu.VMEM((8, TILE), F32),
            pltpu.VMEM((others, 8, TILE), F32),
            pltpu.VMEM((tiles, TILE, 3 * TILE), BF16),
            pltpu.VMEM((tiles, TILE, 3 * TILE), BF16),
            pltpu.VMEM((SWEEPS, (tiles + 1) * TILE, traits), BF16),
            pltpu.VMEM((SWEEPS, (tiles + 1) * TILE, traits), BF16),
            pltpu.VMEM((TILE, TILE), BF16),
            pltpu.VMEM((TILE, TILE), BF16),
            pltpu.VMEM((TILE, traits), F32),
            pltpu.VMEM((2, TILE, traits), BF16),
            pltpu.VMEM((2, TILE, traits), BF16),
            pltpu.VMEM((8, TILE), F32),
            pltpu.VMEM((8, TILE), F32),
            pltpu.VMEM((SWEEPS, TILE, traits), BF16),
            pltpu.VMEM((SWEEPS, TILE, traits), BF16),
            dma((tiles + 3,)),
            dma((2, CHUNKS)),
            dma((2, CHUNKS)),
            dma((others, tiles + 3)),
            dma((others, tiles + 3)),
            dma((3,)),
            dma((3,)),
            dma((SWEEPS, BACK_LAST)),
            dma((SWEEPS, BACK_LAST)),
        ],
        compiler_params=pltpu.CompilerParams(
            collective_id=0, has_side_effects=True, vmem_limit_bytes=VMEM_BYTES
        ),
    )(*(
        pltpu.with_memory_space_constraint(array, pltpu.HBM)
        for array in (genotypes, marginal, start_effects, thresholds[None, :])
    ))


def solution(mesh):
    in_specs = (P("samp", "var"), P("var", "samp"), P("var", "samp"), P("samp"))
    out_specs = P("var", "samp")
    return jax.shard_map(local, mesh=mesh, in_specs=in_specs, out_specs=out_specs, check_vma=False)
```

```python
import functools

import jax
import jax.numpy as jnp
from jax import lax
from jax.experimental import pallas as pl
from jax.experimental.pallas import tpu as pltpu
from jax.sharding import PartitionSpec as P

TILE = 256
HALF = TILE // 2
SWEEPS = 2
CHUNKS = 4
BACK_FIRST = 2
BACK_LAST = 4
TINY = 2.0**-126
VMEM_BYTES = 40 * 1024 * 1024
LD_SCALE = 1024.0

shrinkage = 0.2
MESH = pl.DeviceIdType.MESH
F32 = jnp.float32
BF16 = jnp.bfloat16


def encode(value):
    square = value * value
    fourth = square * square
    eighth = fourth * fourth
    return jnp.where(value < 0, -eighth, eighth).astype(BF16)


def decode(code):
    code = code.astype(F32)
    size = jnp.abs(code)
    fourth_root = lax.rsqrt(lax.rsqrt(jnp.maximum(size, TINY)))
    root = jnp.where(size < TINY, 0.0, fourth_root * lax.rsqrt(fourth_root))
    return jnp.where(code < 0, -root, root)


def encode_wide(value):
    square = value * value
    fourth = square * square
    return jnp.where(value < 0, -fourth, fourth).astype(BF16)


def decode_wide(code):
    code = code.astype(F32)
    size = jnp.abs(code)
    root = jnp.where(size < TINY, 0.0, lax.rsqrt(lax.rsqrt(jnp.maximum(size, TINY))))
    return jnp.where(code < 0, -root, root)


def split(value):
    high = value.astype(BF16)
    return high, (value - high.astype(F32)).astype(BF16)


def iota_pair(size):
    row = lax.broadcasted_iota(jnp.int32, (size, size), 0)
    col = lax.broadcasted_iota(jnp.int32, (size, size), 1)
    return row, col


def pack_symmetric(tile):
    row, col = iota_pair(HALF)
    mixed = jnp.where(row < col, tile[:HALF, :HALF], tile[HALF:, HALF:])
    return jnp.concatenate([mixed, tile[:HALF, HALF:]], axis=1)


def unpack_symmetric(packed):
    row, col = iota_pair(HALF)
    mixed, corner = packed[:, :HALF], packed[:, HALF:]
    upper = jnp.where(row < col, mixed, 0.0)
    lower = jnp.where(row > col, mixed, 0.0)
    first = jnp.concatenate([upper + upper.T, corner], axis=1)
    second = jnp.concatenate([corner.T, lower + lower.T], axis=1)
    return jnp.concatenate([first, second], axis=0)


def gram(left, right):
    return lax.dot_general(left, right, (((0,), (0,)), ((), ())), preferred_element_type=F32)


def kernel(
    tiles, var_size, samp_size, inv_total,
    geno_hbm, marg_hbm, start_hbm, limit_hbm, out,
    geno, halo, marg, start, limit_row, own, code, got, diag, diag_got,
    band_hi, band_lo, eff_hi, eff_lo, cross_hi, cross_lo, first_term,
    early_code, early_got, tail_diag, tail_got, back_code, back_got,
    load_sem, geno_send, geno_recv, part_send, part_recv,
    early_send, early_recv, back_send, back_recv,
):
    var = lax.axis_index("var")
    samp = lax.axis_index("samp")
    has_prev = var > 0
    has_next = var < var_size - 1
    prev, following = var - 1, var + 1
    peers = [lax.rem(samp + k, samp_size) for k in range(1, samp_size)]
    last = tiles - 1
    tail = slice(last * TILE, tiles * TILE)

    step = HALF + TILE
    cross_at = tiles * step - TILE
    halves = range(2)
    diag_message = tiles + 2

    loads = []
    for t in range(tiles):
        cols = pl.ds(t * TILE, TILE)
        loads.append(pltpu.make_async_copy(geno_hbm.at[:, cols], geno.at[:, cols], load_sem.at[t]))
    loads.append(pltpu.make_async_copy(start_hbm, start, load_sem.at[tiles]))
    loads.append(pltpu.make_async_copy(marg_hbm, marg, load_sem.at[tiles + 1]))
    loads.append(pltpu.make_async_copy(limit_hbm, limit_row, load_sem.at[tiles + 2]))
    for copy in loads:
        copy.start()

    barrier = pltpu.get_barrier_semaphore()

    @pl.when(has_prev)
    def _():
        pl.semaphore_signal(barrier, inc=1, device_id={"var": prev}, device_id_type=MESH)

    @pl.when(has_next)
    def _():
        pl.semaphore_signal(barrier, inc=1, device_id={"var": following}, device_id_type=MESH)

    for peer in peers:
        pl.semaphore_signal(barrier, inc=1, device_id={"samp": peer}, device_id_type=MESH)
    pl.semaphore_wait(
        barrier, len(peers) + has_prev.astype(jnp.int32) + has_next.astype(jnp.int32)
    )

    depth = geno.shape[0] // CHUNKS
    chunks = [(half, chunk) for half in halves for chunk in range(CHUNKS)]

    def geno_copy(half, chunk):
        rows = pl.ds(chunk * depth, depth)
        return pltpu.make_async_remote_copy(
            src_ref=geno_hbm.at[rows, pl.ds(last * TILE + half * HALF, HALF)],
            dst_ref=halo.at[rows, pl.ds(half * HALF, HALF)],
            send_sem=geno_send.at[half, chunk], recv_sem=geno_recv.at[half, chunk],
            device_id={"var": following}, device_id_type=MESH,
        )

    @pl.when(has_next)
    def _():
        for half, chunk in chunks:
            geno_copy(half, chunk).start()

    def part_copy(k, message):
        if message == diag_message:
            src, dst = diag, diag_got.at[k]
        else:
            if message < tiles:
                rows = pl.ds(message * step, HALF if message == last else step)
            else:
                rows = pl.ds(cross_at + (message - tiles) * HALF, HALF)
            src, dst = code.at[rows], got.at[k, rows]
        return pltpu.make_async_remote_copy(
            src_ref=src, dst_ref=dst,
            send_sem=part_send.at[k, message], recv_sem=part_recv.at[k, message],
            device_id={"samp": peers[k]}, device_id_type=MESH,
        )

    def send_part(message):
        for k in range(len(peers)):
            part_copy(k, message).start()

    def take_part(message):
        for k in range(len(peers)):
            part_copy(k, message).wait_recv()

    diag[...] = jnp.zeros_like(diag)
    row, col = iota_pair(TILE)
    on_diagonal = row == col

    for t in range(tiles):
        if t == 0:
            loads[0].wait()
        if t + 1 < tiles:
            loads[t + 1].wait()
        reach = min(t + 2, tiles) * TILE
        product = gram(geno[:, t * TILE : (t + 1) * TILE], geno[:, t * TILE : reach])
        product = product * (inv_total * LD_SCALE)
        block = product[:, :TILE]
        diag[pl.ds(t, 1), :] = jnp.sum(jnp.where(on_diagonal, block, 0.0), axis=0, keepdims=True)
        begin = t * step
        packed = pack_symmetric(block)
        own[begin : begin + HALF] = packed
        code[begin : begin + HALF] = encode(packed)
        if t + 1 < tiles:
            beside = product[:, TILE:]
            own[begin + HALF : begin + step] = beside
            code[begin + HALF : begin + step] = encode(beside)
        if t == last:
            send_part(diag_message)
        send_part(t)

    for copy in loads[tiles:]:
        copy.wait()

    def place(sweep, slot, value, first=0):
        begin = slot * TILE + first
        high, low = split(value)
        eff_hi[sweep, begin : begin + value.shape[0]] = high
        eff_lo[sweep, begin : begin + value.shape[0]] = low

    early = [(early_code.at[k], early_got.at[k]) for k in range(2)] + [(tail_diag, tail_got)]

    def early_copy(k):
        src, dst = early[k]
        return pltpu.make_async_remote_copy(
            src_ref=src, dst_ref=dst, send_sem=early_send.at[k], recv_sem=early_recv.at[k],
            device_id={"var": following}, device_id_type=MESH,
        )

    def send_early(k):
        @pl.when(has_next)
        def _():
            early_copy(k).start()

    early_code[0] = encode(start[tail])
    send_early(0)
    for t in range(tiles):
        place(0, t + 1, start[t * TILE : (t + 1) * TILE])

    def summed(begin, size):
        value = own[begin : begin + size]
        for k in range(len(peers)):
            value = value + decode(got[k, begin : begin + size])
        return value

    def put(tile, slot, value, first=0):
        high, low = split(value)
        begin = slot * TILE + first
        band_hi[tile, :, begin : begin + value.shape[1]] = high
        band_lo[tile, :, begin : begin + value.shape[1]] = low

    dot = functools.partial(jnp.dot, preferred_element_type=F32)

    def applied(sweep, tile, first, count):
        across = slice(first * TILE, (first + count) * TILE)
        rows = slice((tile + first) * TILE, (tile + first + count) * TILE)
        high, low = band_hi[tile, :, across], band_lo[tile, :, across]
        near, rest = eff_hi[sweep, rows], eff_lo[sweep, rows]
        return dot(high, near) + (dot(high, rest) + dot(low, near))

    def add_tile(t):
        take_part(t)
        begin = t * step
        put(t, 1, unpack_symmetric(summed(begin, HALF)) * (1.0 / LD_SCALE))
        if t + 1 < tiles:
            beside = summed(begin + HALF, TILE) * (1.0 / LD_SCALE)
            put(t, 2, beside)
            put(t + 1, 0, beside.T)

    def cross_step(half, now):
        @pl.when(jnp.logical_and(has_prev, now))
        def _():
            crossing = jnp.zeros((HALF, TILE), F32)
            for chunk in range(CHUNKS):
                rows = slice(chunk * depth, (chunk + 1) * depth)
                geno_copy(half, chunk).wait_recv()
                crossing = crossing + gram(
                    halo[rows, half * HALF : (half + 1) * HALF], geno[rows, :TILE]
                )
            crossing = crossing * (inv_total * LD_SCALE)
            begin = cross_at + half * HALF
            own[begin : begin + HALF] = crossing
            code[begin : begin + HALF] = encode(crossing)
            send_part(tiles + half)

    nearby = lax.rem(var, 2) == 1
    far = jnp.logical_not(nearby)
    for half in halves:
        cross_step(half, nearby)
    add_tile(0)
    cross_step(0, far)
    for t in range(1, tiles):
        add_tile(t)
    cross_step(1, far)
    take_part(diag_message)

    def keep_of(whole):
        column = jnp.sum(jnp.where(on_diagonal, whole, 0.0), axis=1, keepdims=True) * (1.0 / LD_SCALE)
        return 1.0 / ((1.0 - shrinkage) * column + shrinkage)

    keep = []
    for t in range(tiles):
        whole = diag[pl.ds(t, 1), :]
        for k in range(len(peers)):
            whole = whole + diag_got[k, pl.ds(t, 1), :]
        keep.append(keep_of(whole))
        if t == last:
            tail_diag[...] = jnp.broadcast_to(whole, tail_diag.shape)
    limit = limit_row[...]

    def adjust(tile, combined, rows=slice(0, TILE)):
        shift = slice(tile * TILE + rows.start, tile * TILE + rows.stop)
        return (marg[shift] - (1.0 - shrinkage) * combined) * keep[tile][rows]

    def soften(value, scale):
        bound = limit * scale
        return value - jnp.clip(value, -bound, bound)

    def finish(tile, combined, rows=slice(0, TILE)):
        return soften(adjust(tile, combined, rows), keep[tile][rows])

    near_last = applied(0, last, 0, 2)
    early_code[1] = encode(adjust(last, near_last))
    send_early(2)
    send_early(1)
    near_first = applied(0, 0, 1, 2)
    sizes = (BACK_FIRST, BACK_LAST)
    places = [(sweep, piece) for sweep in range(SWEEPS) for piece in range(sizes[sweep])]

    def piece_rows(sweep, piece):
        size = TILE // sizes[sweep]
        return slice(piece * size, (piece + 1) * size)

    def back_copy(sweep, piece):
        rows = piece_rows(sweep, piece)
        return pltpu.make_async_remote_copy(
            src_ref=back_code.at[sweep, pl.ds(rows.start, rows.stop - rows.start)],
            dst_ref=back_got.at[sweep, pl.ds(rows.start, rows.stop - rows.start)],
            send_sem=back_send.at[sweep, piece], recv_sem=back_recv.at[sweep, piece],
            device_id={"var": prev}, device_id_type=MESH,
        )

    def across(sweep, rows):
        near, rest = eff_hi[sweep, TILE : 2 * TILE], eff_lo[sweep, TILE : 2 * TILE]
        high, low = cross_hi[rows], cross_lo[rows]
        return dot(high, near) + (dot(high, rest) + dot(low, near))

    @pl.when(has_prev)
    def _():
        early_copy(0).wait_recv()
        place(0, 0, decode(early_got[0]))
        for half in halves:
            rows = piece_rows(0, half)
            take_part(tiles + half)
            crossing = summed(cross_at + half * HALF, HALF) * (1.0 / LD_SCALE)
            cross_hi[rows], cross_lo[rows] = split(crossing)
            term = across(0, rows)
            first_term[rows] = term
            back_code[0, rows] = encode(term)
            back_copy(0, half).start()
            put(0, 0, crossing.T, half * HALF)

    @pl.when(jnp.logical_not(has_prev))
    def _():
        put(0, 0, jnp.zeros((TILE, TILE), F32))
        for sweep in range(SWEEPS):
            place(sweep, 0, jnp.zeros((TILE, limit.shape[1]), F32))

    place(1, 1, finish(0, near_first + applied(0, 0, 0, 1)))

    @pl.when(has_prev)
    def _():
        for piece in range(BACK_LAST):
            rows = piece_rows(1, piece)
            back_code[1, rows] = encode_wide(across(1, rows))
            back_copy(1, piece).start()
        early_copy(2).wait_recv()
        early_copy(1).wait_recv()
        scale = keep_of(tail_got[pl.ds(0, 1), :])
        value = decode(early_got[1]) - (1.0 - shrinkage) * (first_term[...] * scale)
        place(1, 0, soften(value, scale))

    for t in range(1, last):
        place(1, t + 1, finish(t, applied(0, t, 0, 3)))
    for t in range(last - 1):
        out[t * TILE : (t + 1) * TILE] = finish(t, applied(1, t, 0, 3))
    inner = applied(1, last - 1, 0, 2)
    edge = applied(1, last, 0, 1)

    @pl.when(jnp.logical_not(has_next))
    def _():
        back_got[...] = jnp.zeros_like(back_got)

    for piece in range(BACK_FIRST):
        rows = piece_rows(0, piece)

        @pl.when(has_next)
        def _():
            back_copy(0, piece).wait_recv()

        place(1, tiles, finish(last, near_last[rows] + decode(back_got[0, rows]), rows), rows.start)

    out[(last - 1) * TILE : last * TILE] = finish(last - 1, inner + applied(1, last - 1, 2, 1))
    edge = edge + applied(1, last, 1, 1)

    for k in range(len(peers)):
        for message in list(range(tiles)) + [diag_message]:
            part_copy(k, message).wait_send()

    @pl.when(has_prev)
    def _():
        for k in range(len(peers)):
            for half in halves:
                part_copy(k, tiles + half).wait_send()
        for sweep, piece in places:
            back_copy(sweep, piece).wait_send()

    @pl.when(has_next)
    def _():
        for half, chunk in chunks:
            geno_copy(half, chunk).wait_send()
        for k in range(len(early)):
            early_copy(k).wait_send()

    for piece in range(BACK_LAST):
        rows = piece_rows(1, piece)

        @pl.when(has_next)
        def _():
            back_copy(1, piece).wait_recv()

        combined = edge[rows] + decode_wide(back_got[1, rows])
        out[last * TILE + rows.start : last * TILE + rows.stop] = finish(last, combined, rows)


def local(genotypes, marginal, start_effects, thresholds):
    samples, variants = genotypes.shape
    traits = marginal.shape[1]
    tiles = variants // TILE
    var_size, samp_size = lax.axis_size("var"), lax.axis_size("samp")
    others = samp_size - 1
    rows = tiles * (HALF + TILE)
    dma = pltpu.SemaphoreType.DMA
    body = functools.partial(
        kernel, tiles, var_size, samp_size, 1.0 / (samples * samp_size)
    )
    return pl.pallas_call(
        body,
        out_shape=jax.ShapeDtypeStruct((variants, traits), F32),
        in_specs=[pl.BlockSpec(memory_space=pltpu.HBM)] * 4,
        out_specs=pl.BlockSpec(memory_space=pltpu.VMEM),
        scratch_shapes=[
            pltpu.VMEM((samples, variants), BF16),
            pltpu.VMEM((samples, TILE), BF16),
            pltpu.VMEM((variants, traits), F32),
            pltpu.VMEM((variants, traits), F32),
            pltpu.VMEM((1, traits), F32),
            pltpu.VMEM((rows, TILE), F32),
            pltpu.VMEM((rows, TILE), BF16),
            pltpu.VMEM((others, rows, TILE), BF16),
            pltpu.VMEM((8, TILE), F32),
            pltpu.VMEM((others, 8, TILE), F32),
            pltpu.VMEM((tiles, TILE, 3 * TILE), BF16),
            pltpu.VMEM((tiles, TILE, 3 * TILE), BF16),
            pltpu.VMEM((SWEEPS, (tiles + 1) * TILE, traits), BF16),
            pltpu.VMEM((SWEEPS, (tiles + 1) * TILE, traits), BF16),
            pltpu.VMEM((TILE, TILE), BF16),
            pltpu.VMEM((TILE, TILE), BF16),
            pltpu.VMEM((TILE, traits), F32),
            pltpu.VMEM((2, TILE, traits), BF16),
            pltpu.VMEM((2, TILE, traits), BF16),
            pltpu.VMEM((8, TILE), F32),
            pltpu.VMEM((8, TILE), F32),
            pltpu.VMEM((SWEEPS, TILE, traits), BF16),
            pltpu.VMEM((SWEEPS, TILE, traits), BF16),
            dma((tiles + 3,)),
            dma((2, CHUNKS)),
            dma((2, CHUNKS)),
            dma((others, tiles + 3)),
            dma((others, tiles + 3)),
            dma((3,)),
            dma((3,)),
            dma((SWEEPS, BACK_LAST)),
            dma((SWEEPS, BACK_LAST)),
        ],
        compiler_params=pltpu.CompilerParams(
            collective_id=0, has_side_effects=True, vmem_limit_bytes=VMEM_BYTES
        ),
    )(*(
        pltpu.with_memory_space_constraint(array, pltpu.HBM)
        for array in (genotypes, marginal, start_effects, thresholds[None, :])
    ))


def solution(mesh):
    in_specs = (P("samp", "var"), P("var", "samp"), P("var", "samp"), P("samp"))
    out_specs = P("var", "samp")
    return jax.shard_map(local, mesh=mesh, in_specs=in_specs, out_specs=out_specs, check_vma=False)
```

```python
import functools

import jax
import jax.numpy as jnp
from jax import lax
from jax.experimental import pallas as pl
from jax.experimental.pallas import tpu as pltpu
from jax.sharding import PartitionSpec as P

TILE = 256
HALF = TILE // 2
SWEEPS = 2
CHUNKS = 4
BACK_FIRST = 2
BACK_LAST = 4
TINY = 2.0**-126
VMEM_BYTES = 40 * 1024 * 1024
LD_SCALE = 1024.0

shrinkage = 0.2
MESH = pl.DeviceIdType.MESH
F32 = jnp.float32
BF16 = jnp.bfloat16


def encode(value):
    square = value * value
    fourth = square * square
    eighth = fourth * fourth
    return jnp.where(value < 0, -eighth, eighth).astype(BF16)


def decode(code):
    code = code.astype(F32)
    size = jnp.abs(code)
    fourth_root = lax.rsqrt(lax.rsqrt(jnp.maximum(size, TINY)))
    root = jnp.where(size < TINY, 0.0, fourth_root * lax.rsqrt(fourth_root))
    return jnp.where(code < 0, -root, root)


def encode_wide(value):
    square = value * value
    fourth = square * square
    return jnp.where(value < 0, -fourth, fourth).astype(BF16)


def decode_wide(code):
    code = code.astype(F32)
    size = jnp.abs(code)
    root = jnp.where(size < TINY, 0.0, lax.rsqrt(lax.rsqrt(jnp.maximum(size, TINY))))
    return jnp.where(code < 0, -root, root)


def split(value):
    high = value.astype(BF16)
    return high, (value - high.astype(F32)).astype(BF16)


def iota_pair(size):
    row = lax.broadcasted_iota(jnp.int32, (size, size), 0)
    col = lax.broadcasted_iota(jnp.int32, (size, size), 1)
    return row, col


def pack_symmetric(tile):
    row, col = iota_pair(HALF)
    mixed = jnp.where(row < col, tile[:HALF, :HALF], tile[HALF:, HALF:])
    return jnp.concatenate([mixed, tile[:HALF, HALF:]], axis=1)


def unpack_symmetric(packed):
    row, col = iota_pair(HALF)
    mixed, corner = packed[:, :HALF], packed[:, HALF:]
    upper = jnp.where(row < col, mixed, 0.0)
    lower = jnp.where(row > col, mixed, 0.0)
    first = jnp.concatenate([upper + upper.T, corner], axis=1)
    second = jnp.concatenate([corner.T, lower + lower.T], axis=1)
    return jnp.concatenate([first, second], axis=0)


def gram(left, right):
    return lax.dot_general(left, right, (((0,), (0,)), ((), ())), preferred_element_type=F32)


def kernel(
    tiles, var_size, samp_size, inv_total,
    geno_hbm, marg_hbm, start_hbm, limit_hbm, out,
    geno, halo, marg, start, limit_row, own, code, got, diag, diag_got,
    band_hi, band_lo, eff_hi, eff_lo, cross_hi, cross_lo, first_term,
    early_code, early_got, tail_diag, tail_got, back_code, back_got, near,
    load_sem, geno_send, geno_recv, part_send, part_recv,
    early_send, early_recv, back_send, back_recv,
):
    var = lax.axis_index("var")
    samp = lax.axis_index("samp")
    has_prev = var > 0
    has_next = var < var_size - 1
    prev, following = var - 1, var + 1
    nearby = lax.rem(var, 2) == 1
    far = jnp.logical_not(nearby)

    def both(*terms):
        return functools.reduce(jnp.logical_and, terms)

    peers = [lax.rem(samp + k, samp_size) for k in range(1, samp_size)]
    last = tiles - 1
    tail = slice(last * TILE, tiles * TILE)

    step = HALF + TILE
    cross_at = tiles * step - TILE
    halves = range(2)
    diag_message = tiles + 2

    loads = []
    for t in range(tiles):
        cols = pl.ds(t * TILE, TILE)
        loads.append(pltpu.make_async_copy(geno_hbm.at[:, cols], geno.at[:, cols], load_sem.at[t]))
    loads.append(pltpu.make_async_copy(start_hbm, start, load_sem.at[tiles]))
    loads.append(pltpu.make_async_copy(marg_hbm, marg, load_sem.at[tiles + 1]))
    loads.append(pltpu.make_async_copy(limit_hbm, limit_row, load_sem.at[tiles + 2]))
    for copy in loads:
        copy.start()

    barrier = pltpu.get_barrier_semaphore()

    @pl.when(has_prev)
    def _():
        pl.semaphore_signal(barrier, inc=1, device_id={"var": prev}, device_id_type=MESH)

    @pl.when(has_next)
    def _():
        pl.semaphore_signal(barrier, inc=1, device_id={"var": following}, device_id_type=MESH)

    for peer in peers:
        pl.semaphore_signal(barrier, inc=1, device_id={"samp": peer}, device_id_type=MESH)

    pl.semaphore_wait(
        barrier, len(peers) + has_prev.astype(jnp.int32) + has_next.astype(jnp.int32)
    )

    depth = geno.shape[0] // CHUNKS
    chunks = [(half, chunk) for half in halves for chunk in range(CHUNKS)]

    def geno_copy(half, chunk):
        rows = pl.ds(chunk * depth, depth)
        return pltpu.make_async_remote_copy(
            src_ref=geno_hbm.at[rows, pl.ds(last * TILE + half * HALF, HALF)],
            dst_ref=halo.at[rows, pl.ds(half * HALF, HALF)],
            send_sem=geno_send.at[half, chunk], recv_sem=geno_recv.at[half, chunk],
            device_id={"var": following}, device_id_type=MESH,
        )

    @pl.when(has_next)
    def _():
        for half, chunk in chunks:
            geno_copy(half, chunk).start()

    def part_copy(k, message):
        if message == diag_message:
            src, dst = diag, diag_got.at[k]
        else:
            if message < tiles:
                rows = pl.ds(message * step, HALF if message == last else step)
            else:
                rows = pl.ds(cross_at + (message - tiles) * HALF, HALF)
            src, dst = code.at[rows], got.at[k, rows]
        return pltpu.make_async_remote_copy(
            src_ref=src, dst_ref=dst,
            send_sem=part_send.at[k, message], recv_sem=part_recv.at[k, message],
            device_id={"samp": peers[k]}, device_id_type=MESH,
        )

    def send_part(message):
        for k in range(len(peers)):
            part_copy(k, message).start()

    def take_part(message):
        for k in range(len(peers)):
            part_copy(k, message).wait_recv()

    diag[...] = jnp.zeros_like(diag)
    row, col = iota_pair(TILE)
    on_diagonal = row == col

    for t in range(tiles):
        if t == 0:
            loads[0].wait()
        if t + 1 < tiles:
            loads[t + 1].wait()
        reach = min(t + 2, tiles) * TILE
        product = gram(geno[:, t * TILE : (t + 1) * TILE], geno[:, t * TILE : reach])
        product = product * (inv_total * LD_SCALE)
        block = product[:, :TILE]
        diag[pl.ds(t, 1), :] = jnp.sum(jnp.where(on_diagonal, block, 0.0), axis=0, keepdims=True)
        begin = t * step
        packed = pack_symmetric(block)
        own[begin : begin + HALF] = packed
        code[begin : begin + HALF] = encode(packed)
        if t + 1 < tiles:
            beside = product[:, TILE:]
            own[begin + HALF : begin + step] = beside
            code[begin + HALF : begin + step] = encode(beside)
        if t < last:
            pl.when(far if t == 0 else var >= 0)(functools.partial(send_part, t))

    @pl.when(nearby)
    def _():
        for message in (last, diag_message, 0):
            send_part(message)

    for copy in loads[tiles:]:
        copy.wait()

    def place(sweep, slot, value, first=0):
        begin = slot * TILE + first
        high, low = split(value)
        eff_hi[sweep, begin : begin + value.shape[0]] = high
        eff_lo[sweep, begin : begin + value.shape[0]] = low

    early = [(early_code.at[k], early_got.at[k]) for k in range(2)] + [(tail_diag, tail_got)]

    def early_copy(k):
        src, dst = early[k]
        return pltpu.make_async_remote_copy(
            src_ref=src, dst_ref=dst, send_sem=early_send.at[k], recv_sem=early_recv.at[k],
            device_id={"var": following}, device_id_type=MESH,
        )

    def send_early(k):
        @pl.when(has_next)
        def _():
            early_copy(k).start()

    early_code[0] = encode(start[tail])
    send_early(0)
    for t in range(tiles):
        place(0, t + 1, start[t * TILE : (t + 1) * TILE])

    def summed(begin, size):
        value = own[begin : begin + size]
        for k in range(len(peers)):
            value = value + decode(got[k, begin : begin + size])
        return value

    def put(tile, slot, value, first=0):
        high, low = split(value)
        begin = slot * TILE + first
        band_hi[tile, :, begin : begin + value.shape[1]] = high
        band_lo[tile, :, begin : begin + value.shape[1]] = low

    dot = functools.partial(jnp.dot, preferred_element_type=F32)

    def applied(sweep, tile, first, count):
        across = slice(first * TILE, (first + count) * TILE)
        rows = slice((tile + first) * TILE, (tile + first + count) * TILE)
        high, low = band_hi[tile, :, across], band_lo[tile, :, across]
        near, rest = eff_hi[sweep, rows], eff_lo[sweep, rows]
        return dot(high, near) + (dot(high, rest) + dot(low, near))

    def add_tile(t):
        take_part(t)
        begin = t * step
        put(t, 1, unpack_symmetric(summed(begin, HALF)) * (1.0 / LD_SCALE))
        if t + 1 < tiles:
            beside = summed(begin + HALF, TILE) * (1.0 / LD_SCALE)
            put(t, 2, beside)
            put(t + 1, 0, beside.T)

    def cross_step(half, now):
        @pl.when(jnp.logical_and(has_prev, now))
        def _():
            crossing = jnp.zeros((HALF, TILE), F32)
            for chunk in range(CHUNKS):
                rows = slice(chunk * depth, (chunk + 1) * depth)
                geno_copy(half, chunk).wait_recv()
                crossing = crossing + gram(
                    halo[rows, half * HALF : (half + 1) * HALF], geno[rows, :TILE]
                )
            crossing = crossing * (inv_total * LD_SCALE)
            begin = cross_at + half * HALF
            own[begin : begin + HALF] = crossing
            code[begin : begin + HALF] = encode(crossing)
            send_part(tiles + half)

    nearby = lax.rem(var, 2) == 1
    far = jnp.logical_not(nearby)
    for half in halves:
        cross_step(half, nearby)
    pl.when(far)(functools.partial(add_tile, 0))
    cross_step(0, far)

    @pl.when(far)
    def _():
        for message in (last, diag_message):
            send_part(message)

    sizes = (BACK_FIRST, BACK_LAST)
    places = [(sweep, piece) for sweep in range(SWEEPS) for piece in range(sizes[sweep])]

    def piece_rows(sweep, piece):
        size = TILE // sizes[sweep]
        return slice(piece * size, (piece + 1) * size)

    def back_copy(sweep, piece):
        rows = piece_rows(sweep, piece)
        return pltpu.make_async_remote_copy(
            src_ref=back_code.at[sweep, pl.ds(rows.start, rows.stop - rows.start)],
            dst_ref=back_got.at[sweep, pl.ds(rows.start, rows.stop - rows.start)],
            send_sem=back_send.at[sweep, piece], recv_sem=back_recv.at[sweep, piece],
            device_id={"var": prev}, device_id_type=MESH,
        )

    def across(sweep, rows):
        near, rest = eff_hi[sweep, TILE : 2 * TILE], eff_lo[sweep, TILE : 2 * TILE]
        high, low = cross_hi[rows], cross_lo[rows]
        return dot(high, near) + (dot(high, rest) + dot(low, near))

    def first_back(half):
        rows = piece_rows(0, half)
        take_part(tiles + half)
        crossing = summed(cross_at + half * HALF, HALF) * (1.0 / LD_SCALE)
        cross_hi[rows], cross_lo[rows] = split(crossing)
        term = across(0, rows)
        first_term[rows] = term
        back_code[0, rows] = encode(term)
        back_copy(0, half).start()
        put(0, 0, crossing.T, half * HALF)

    cross_step(1, far)

    @pl.when(both(has_prev, far))
    def _():
        first_back(0)

    take_part(diag_message)

    def keep_of(whole):
        column = jnp.sum(jnp.where(on_diagonal, whole, 0.0), axis=1, keepdims=True) * (1.0 / LD_SCALE)
        return 1.0 / ((1.0 - shrinkage) * column + shrinkage)

    keep = []
    for t in range(tiles):
        whole = diag[pl.ds(t, 1), :]
        for k in range(len(peers)):
            whole = whole + diag_got[k, pl.ds(t, 1), :]
        keep.append(keep_of(whole))
        if t == last:
            tail_diag[...] = jnp.broadcast_to(whole, tail_diag.shape)
    send_early(2)
    limit = limit_row[...]

    def adjust(tile, combined, rows=slice(0, TILE)):
        shift = slice(tile * TILE + rows.start, tile * TILE + rows.stop)
        return (marg[shift] - (1.0 - shrinkage) * combined) * keep[tile][rows]

    def soften(value, scale):
        bound = limit * scale
        return value - jnp.clip(value, -bound, bound)

    def finish(tile, combined, rows=slice(0, TILE)):
        return soften(adjust(tile, combined, rows), keep[tile][rows])

    for t in range(last, 0, -1):
        add_tile(t)
    near[1] = applied(0, last, 0, 2)
    early_code[1] = encode(adjust(last, near[1]))
    send_early(1)
    pl.when(nearby)(functools.partial(add_tile, 0))
    near[0] = applied(0, 0, 1, 2)

    @pl.when(both(has_prev, nearby))
    def _():
        first_back(0)

    @pl.when(has_prev)
    def _():
        first_back(1)
        early_copy(0).wait_recv()
        place(0, 0, decode(early_got[0]))

    @pl.when(jnp.logical_not(has_prev))
    def _():
        put(0, 0, jnp.zeros((TILE, TILE), F32))
        for sweep in range(SWEEPS):
            place(sweep, 0, jnp.zeros((TILE, limit.shape[1]), F32))

    place(1, 1, finish(0, near[0] + applied(0, 0, 0, 1)))

    @pl.when(has_prev)
    def _():
        for piece in range(BACK_LAST):
            rows = piece_rows(1, piece)
            back_code[1, rows] = encode_wide(across(1, rows))
            back_copy(1, piece).start()

    for t in range(1, last):
        place(1, t + 1, finish(t, applied(0, t, 0, 3)))

    near[0] = applied(1, 0, 1, 2)
    for t in range(1, last - 1):
        out[t * TILE : (t + 1) * TILE] = finish(t, applied(1, t, 0, 3))
    inner = applied(1, last - 1, 0, 2)
    edge = applied(1, last, 0, 1)

    @pl.when(jnp.logical_not(has_next))
    def _():
        back_got[...] = jnp.zeros_like(back_got)

    for piece in range(BACK_FIRST):
        rows = piece_rows(0, piece)

        @pl.when(has_next)
        def _():
            back_copy(0, piece).wait_recv()

        place(1, tiles, finish(last, near[1, rows] + decode(back_got[0, rows]), rows), rows.start)

    out[(last - 1) * TILE : last * TILE] = finish(last - 1, inner + applied(1, last - 1, 2, 1))
    edge = edge + applied(1, last, 1, 1)

    @pl.when(has_prev)
    def _():
        early_copy(2).wait_recv()
        early_copy(1).wait_recv()
        scale = keep_of(tail_got[pl.ds(0, 1), :])
        value = decode(early_got[1]) - (1.0 - shrinkage) * (first_term[...] * scale)
        place(1, 0, soften(value, scale))

    out[:TILE] = finish(0, near[0] + applied(1, 0, 0, 1))

    for k in range(len(peers)):
        for message in list(range(tiles)) + [diag_message]:
            part_copy(k, message).wait_send()

    @pl.when(has_next)
    def _():
        for half, chunk in chunks:
            geno_copy(half, chunk).wait_send()
        for k in range(len(early)):
            early_copy(k).wait_send()

    for piece in range(BACK_LAST):
        rows = piece_rows(1, piece)

        @pl.when(has_next)
        def _():
            back_copy(1, piece).wait_recv()

        combined = edge[rows] + decode_wide(back_got[1, rows])
        out[last * TILE + rows.start : last * TILE + rows.stop] = finish(last, combined, rows)


    @pl.when(has_prev)
    def _():
        for k in range(len(peers)):
            for half in halves:
                part_copy(k, tiles + half).wait_send()
        for sweep, piece in places:
            back_copy(sweep, piece).wait_send()


def local(genotypes, marginal, start_effects, thresholds):
    samples, variants = genotypes.shape
    traits = marginal.shape[1]
    tiles = variants // TILE
    var_size, samp_size = lax.axis_size("var"), lax.axis_size("samp")
    others = samp_size - 1
    rows = tiles * (HALF + TILE)
    dma = pltpu.SemaphoreType.DMA
    body = functools.partial(
        kernel, tiles, var_size, samp_size, 1.0 / (samples * samp_size)
    )
    return pl.pallas_call(
        body,
        out_shape=jax.ShapeDtypeStruct((variants, traits), F32),
        in_specs=[pl.BlockSpec(memory_space=pltpu.HBM)] * 4,
        out_specs=pl.BlockSpec(memory_space=pltpu.VMEM),
        scratch_shapes=[
            pltpu.VMEM((samples, variants), BF16),
            pltpu.VMEM((samples, TILE), BF16),
            pltpu.VMEM((variants, traits), F32),
            pltpu.VMEM((variants, traits), F32),
            pltpu.VMEM((1, traits), F32),
            pltpu.VMEM((rows, TILE), F32),
            pltpu.VMEM((rows, TILE), BF16),
            pltpu.VMEM((others, rows, TILE), BF16),
            pltpu.VMEM((8, TILE), F32),
            pltpu.VMEM((others, 8, TILE), F32),
            pltpu.VMEM((tiles, TILE, 3 * TILE), BF16),
            pltpu.VMEM((tiles, TILE, 3 * TILE), BF16),
            pltpu.VMEM((SWEEPS, (tiles + 1) * TILE, traits), BF16),
            pltpu.VMEM((SWEEPS, (tiles + 1) * TILE, traits), BF16),
            pltpu.VMEM((TILE, TILE), BF16),
            pltpu.VMEM((TILE, TILE), BF16),
            pltpu.VMEM((TILE, traits), F32),
            pltpu.VMEM((2, TILE, traits), BF16),
            pltpu.VMEM((2, TILE, traits), BF16),
            pltpu.VMEM((8, TILE), F32),
            pltpu.VMEM((8, TILE), F32),
            pltpu.VMEM((SWEEPS, TILE, traits), BF16),
            pltpu.VMEM((SWEEPS, TILE, traits), BF16),
            pltpu.VMEM((2, TILE, traits), F32),
            dma((tiles + 3,)),
            dma((2, CHUNKS)),
            dma((2, CHUNKS)),
            dma((others, tiles + 3)),
            dma((others, tiles + 3)),
            dma((3,)),
            dma((3,)),
            dma((SWEEPS, BACK_LAST)),
            dma((SWEEPS, BACK_LAST)),
        ],
        compiler_params=pltpu.CompilerParams(
            collective_id=0, has_side_effects=True, vmem_limit_bytes=VMEM_BYTES
        ),
    )(*(
        pltpu.with_memory_space_constraint(array, pltpu.HBM)
        for array in (genotypes, marginal, start_effects, thresholds[None, :])
    ))


def solution(mesh):
    in_specs = (P("samp", "var"), P("var", "samp"), P("var", "samp"), P("samp"))
    out_specs = P("var", "samp")
    return jax.shard_map(local, mesh=mesh, in_specs=in_specs, out_specs=out_specs, check_vma=False)
```

```python
import functools

import jax
import jax.numpy as jnp
from jax import lax
from jax.experimental import pallas as pl
from jax.experimental.pallas import tpu as pltpu
from jax.sharding import PartitionSpec as P

TILE = 256
HALF = TILE // 2
SWEEPS = 2
QUARTER = TILE // 4
TINY = 2.0**-126
VMEM_BYTES = 40 * 1024 * 1024
LD_SCALE = 1024.0

shrinkage = 0.2
MESH = pl.DeviceIdType.MESH
F32 = jnp.float32
BF16 = jnp.bfloat16


def encode(value):
    square = value * value
    fourth = square * square
    eighth = fourth * fourth
    return jnp.where(value < 0, -eighth, eighth).astype(BF16)


def decode(code):
    code = code.astype(F32)
    size = jnp.abs(code)
    fourth_root = lax.rsqrt(lax.rsqrt(jnp.maximum(size, TINY)))
    root = jnp.where(size < TINY, 0.0, fourth_root * lax.rsqrt(fourth_root))
    return jnp.where(code < 0, -root, root)


def encode_wide(value):
    square = value * value
    fourth = square * square
    return jnp.where(value < 0, -fourth, fourth).astype(BF16)


def decode_wide(code):
    code = code.astype(F32)
    size = jnp.abs(code)
    root = jnp.where(size < TINY, 0.0, lax.rsqrt(lax.rsqrt(jnp.maximum(size, TINY))))
    return jnp.where(code < 0, -root, root)


def split(value):
    high = value.astype(BF16)
    return high, (value - high.astype(F32)).astype(BF16)


def iota_pair(size):
    row = lax.broadcasted_iota(jnp.int32, (size, size), 0)
    col = lax.broadcasted_iota(jnp.int32, (size, size), 1)
    return row, col


def pack_symmetric(tile):
    row, col = iota_pair(HALF)
    mixed = jnp.where(row < col, tile[:HALF, :HALF], tile[HALF:, HALF:])
    return jnp.concatenate([mixed, tile[:HALF, HALF:]], axis=1)


def unpack_symmetric(packed):
    row, col = iota_pair(HALF)
    mixed, corner = packed[:, :HALF], packed[:, HALF:]
    upper = jnp.where(row < col, mixed, 0.0)
    lower = jnp.where(row > col, mixed, 0.0)
    first = jnp.concatenate([upper + upper.T, corner], axis=1)
    second = jnp.concatenate([corner.T, lower + lower.T], axis=1)
    return jnp.concatenate([first, second], axis=0)


def gram(left, right):
    return lax.dot_general(left, right, (((0,), (0,)), ((), ())), preferred_element_type=F32)


def kernel(
    tiles, var_size, samp_size, inv_total,
    geno_hbm, marg_hbm, start_hbm, limit_hbm, out,
    geno, halo, table, limit_row, own, code, got, diag, diag_got,
    band_hi, band_lo, eff_hi, eff_lo, cross_hi, cross_lo, first_term,
    early_code, early_got, tail_diag, tail_got, back_code, back_got, near,
    load_sem, geno_send, geno_recv, part_send, part_recv,
    early_send, early_recv, back_send, back_recv,
):
    var = lax.axis_index("var")
    samp = lax.axis_index("samp")
    has_prev = var > 0
    has_next = var < var_size - 1
    prev, following = var - 1, var + 1
    nearby = lax.rem(var, 2) == 1
    far = jnp.logical_not(nearby)

    def both(*terms):
        return functools.reduce(jnp.logical_and, terms)

    peers = [lax.rem(samp + k, samp_size) for k in range(1, samp_size)]
    last = tiles - 1
    tail = slice(last * TILE, tiles * TILE)

    step = HALF + TILE
    cross_at = tiles * step - TILE
    total_rows = cross_at + TILE
    halves = range(2)
    cross_spans = [(0, HALF), (HALF, HALF)]
    diag_message = tiles + len(cross_spans)
    marg, start = table.at[0], table.at[1]
    first_cols = pl.ds(0, 2 * TILE)
    other_cols = pl.ds(2 * TILE, (tiles - 2) * TILE)
    loads = [
        pltpu.make_async_copy(geno_hbm.at[:, first_cols], geno.at[:, first_cols], load_sem.at[0]),
        pltpu.make_async_copy(geno_hbm.at[:, other_cols], geno.at[:, other_cols], load_sem.at[1]),
        pltpu.make_async_copy(start_hbm, start, load_sem.at[2]),
        pltpu.make_async_copy(marg_hbm, marg, load_sem.at[2]),
        pltpu.make_async_copy(limit_hbm, limit_row, load_sem.at[3]),
    ]

    barrier = pltpu.get_barrier_semaphore()

    @pl.when(has_prev)
    def _():
        pl.semaphore_signal(barrier, inc=1, device_id={"var": prev}, device_id_type=MESH)

    @pl.when(has_next)
    def _():
        pl.semaphore_signal(barrier, inc=1, device_id={"var": following}, device_id_type=MESH)

    for peer in peers:
        pl.semaphore_signal(barrier, inc=1, device_id={"samp": peer}, device_id_type=MESH)

    for copy in loads:
        copy.start()

    pl.semaphore_wait(
        barrier, len(peers) + has_prev.astype(jnp.int32) + has_next.astype(jnp.int32)
    )

    depth = geno.shape[0]
    cut = depth - depth // 4
    geno_spans = [(0, 0, depth), (1, 0, cut), (1, cut, depth)]

    def geno_copy(index):
        half, begin, end = geno_spans[index]
        rows = pl.ds(begin, end - begin)
        return pltpu.make_async_remote_copy(
            src_ref=geno_hbm.at[rows, pl.ds(last * TILE + half * HALF, HALF)],
            dst_ref=halo.at[rows, pl.ds(half * HALF, HALF)],
            send_sem=geno_send, recv_sem=geno_recv.at[index],
            device_id={"var": following}, device_id_type=MESH,
        )

    def geno_sent():
        return pltpu.make_async_remote_copy(
            src_ref=geno_hbm.at[:, pl.ds(last * TILE, TILE)], dst_ref=halo,
            send_sem=geno_send, recv_sem=geno_recv.at[0],
            device_id={"var": following}, device_id_type=MESH,
        )

    @pl.when(has_next)
    def _():
        for index in range(len(geno_spans)):
            geno_copy(index).start()

    def code_copy(k, begin, end, arrival):
        rows = pl.ds(begin, end - begin)
        return pltpu.make_async_remote_copy(
            src_ref=code.at[rows], dst_ref=got.at[k, rows],
            send_sem=part_send.at[k, 0], recv_sem=part_recv.at[k, arrival],
            device_id={"samp": peers[k]}, device_id_type=MESH,
        )

    def diag_copy(k):
        return pltpu.make_async_remote_copy(
            src_ref=diag, dst_ref=diag_got.at[k],
            send_sem=part_send.at[k, 1], recv_sem=part_recv.at[k, 2 + len(cross_spans)],
            device_id={"samp": peers[k]}, device_id_type=MESH,
        )

    def part_copy(k, message):
        if message == diag_message:
            return diag_copy(k)
        if message < tiles:
            begin = message * step
            return code_copy(k, begin, min(begin + step, cross_at), min(message, 1))
        first, size = cross_spans[message - tiles]
        return code_copy(k, cross_at + first, cross_at + first + size, 2 + message - tiles)

    def send_part(message):
        for k in range(len(peers)):
            part_copy(k, message).start()

    def take_part(message):
        for k in range(len(peers)):
            if 0 < message < tiles:
                code_copy(k, step, cross_at, 1).wait_recv()
            else:
                part_copy(k, message).wait_recv()

    diag[...] = jnp.zeros_like(diag)
    row, col = iota_pair(TILE)
    on_diagonal = row == col

    for t in range(tiles):
        if t < 2:
            loads[t].wait()
        reach = min(t + 2, tiles) * TILE
        product = gram(geno[:, t * TILE : (t + 1) * TILE], geno[:, t * TILE : reach])
        product = product * (inv_total * LD_SCALE)
        block = product[:, :TILE]
        diag[pl.ds(t, 1), :] = jnp.sum(jnp.where(on_diagonal, block, 0.0), axis=0, keepdims=True)
        begin = t * step
        packed = pack_symmetric(block)
        own[begin : begin + HALF] = packed
        code[begin : begin + HALF] = encode(packed)
        if t + 1 < tiles:
            beside = product[:, TILE:]
            own[begin + HALF : begin + step] = beside
            code[begin + HALF : begin + step] = encode(beside)
        if t < last:
            pl.when(far if t == 0 else var >= 0)(functools.partial(send_part, t))

    @pl.when(nearby)
    def _():
        for message in (last, diag_message, 0):
            send_part(message)

    pltpu.make_async_copy(table, table, load_sem.at[2]).wait()
    loads[4].wait()

    def place(sweep, slot, value, first=0):
        begin = slot * TILE + first
        high, low = split(value)
        eff_hi[sweep, begin : begin + value.shape[0]] = high
        eff_lo[sweep, begin : begin + value.shape[0]] = low

    early = [(early_code.at[k], early_got.at[k], 0) for k in range(2)] + [(tail_diag, tail_got, 1)]

    def early_copy(k):
        src, dst, departure = early[k]
        return pltpu.make_async_remote_copy(
            src_ref=src, dst_ref=dst, send_sem=early_send.at[departure], recv_sem=early_recv.at[k],
            device_id={"var": following}, device_id_type=MESH,
        )

    def early_sent():
        return pltpu.make_async_remote_copy(
            src_ref=early_code, dst_ref=early_got, send_sem=early_send.at[0], recv_sem=early_recv.at[0],
            device_id={"var": following}, device_id_type=MESH,
        )

    def send_early(k):
        @pl.when(has_next)
        def _():
            early_copy(k).start()

    early_code[0] = encode(start[tail])
    send_early(0)
    for t in range(tiles):
        place(0, t + 1, start[t * TILE : (t + 1) * TILE])

    def summed(begin, size):
        value = own[begin : begin + size]
        for k in range(len(peers)):
            value = value + decode(got[k, begin : begin + size])
        return value

    def put(tile, slot, value, first=0):
        high, low = split(value)
        begin = slot * TILE + first
        band_hi[tile, :, begin : begin + value.shape[1]] = high
        band_lo[tile, :, begin : begin + value.shape[1]] = low

    dot = functools.partial(jnp.dot, preferred_element_type=F32)

    def applied(sweep, tile, first, count):
        across = slice(first * TILE, (first + count) * TILE)
        rows = slice((tile + first) * TILE, (tile + first + count) * TILE)
        high, low = band_hi[tile, :, across], band_lo[tile, :, across]
        near, rest = eff_hi[sweep, rows], eff_lo[sweep, rows]
        return dot(high, near) + (dot(high, rest) + dot(low, near))

    def add_tile(t):
        begin = t * step
        put(t, 1, unpack_symmetric(summed(begin, HALF)) * (1.0 / LD_SCALE))
        if t + 1 < tiles:
            beside = summed(begin + HALF, TILE) * (1.0 / LD_SCALE)
            put(t, 2, beside)
            put(t + 1, 0, beside.T)

    def cross_step(half, now):
        @pl.when(jnp.logical_and(has_prev, now))
        def _():
            begin = cross_at + half * HALF
            for index, (side, first, end) in enumerate(geno_spans):
                if side == half:
                    geno_copy(index).wait_recv()
                    crossing = gram(
                        halo[first:end, half * HALF : (half + 1) * HALF], geno[first:end, :TILE]
                    )
                    crossing = crossing * (inv_total * LD_SCALE)
                    if first > 0:
                        crossing = crossing + own[begin : begin + HALF]
                    own[begin : begin + HALF] = crossing
            code[begin : begin + HALF] = encode(crossing)
            for piece, (first, size) in enumerate(cross_spans):
                if first // HALF == half:
                    send_part(tiles + piece)

    for half in halves:
        cross_step(half, nearby)
    def start_first():
        take_part(0)
        add_tile(0)
        near[0] = applied(0, 0, 1, 2)

    cross_step(0, far)

    @pl.when(far)
    def _():
        for message in (last, diag_message):
            send_part(message)
        start_first()

    back_spans = [cross_spans, [(k * QUARTER, QUARTER) for k in range(4)]]

    def back_copy(sweep, first, size, arrival):
        rows = pl.ds(first, size)
        return pltpu.make_async_remote_copy(
            src_ref=back_code.at[sweep, rows], dst_ref=back_got.at[sweep, rows],
            send_sem=back_send, recv_sem=back_recv.at[arrival],
            device_id={"var": prev}, device_id_type=MESH,
        )

    def back_sent():
        return pltpu.make_async_remote_copy(
            src_ref=back_code, dst_ref=back_got, send_sem=back_send, recv_sem=back_recv.at[0],
            device_id={"var": prev}, device_id_type=MESH,
        )

    def across(sweep, rows):
        near, rest = eff_hi[sweep, TILE : 2 * TILE], eff_lo[sweep, TILE : 2 * TILE]
        high, low = cross_hi[rows], cross_lo[rows]
        return dot(high, near) + (dot(high, rest) + dot(low, near))

    def first_back(piece):
        first, size = cross_spans[piece]
        rows = slice(first, first + size)
        take_part(tiles + piece)
        crossing = summed(cross_at + first, size) * (1.0 / LD_SCALE)
        cross_hi[rows], cross_lo[rows] = split(crossing)
        term = across(0, rows)
        first_term[rows] = term
        back_code[0, rows] = encode(term)
        back_copy(0, first, size, 0).start()
        put(0, 0, crossing.T, first)

    cross_step(1, far)

    @pl.when(both(has_prev, far))
    def _():
        first_back(0)

    take_part(diag_message)

    def keep_of(whole):
        column = jnp.sum(jnp.where(on_diagonal, whole, 0.0), axis=1, keepdims=True) * (1.0 / LD_SCALE)
        return 1.0 / ((1.0 - shrinkage) * column + shrinkage)

    keep = []
    for t in range(tiles):
        whole = diag[pl.ds(t, 1), :]
        for k in range(len(peers)):
            whole = whole + diag_got[k, pl.ds(t, 1), :]
        keep.append(keep_of(whole))
        if t == last:
            tail_diag[...] = jnp.broadcast_to(whole, tail_diag.shape)
    send_early(2)
    limit = limit_row[...]

    def adjust(tile, combined, rows=slice(0, TILE)):
        shift = slice(tile * TILE + rows.start, tile * TILE + rows.stop)
        return (marg[shift] - (1.0 - shrinkage) * combined) * keep[tile][rows]

    def soften(value, scale):
        bound = limit * scale
        return value - jnp.clip(value, -bound, bound)

    def finish(tile, combined, rows=slice(0, TILE)):
        return soften(adjust(tile, combined, rows), keep[tile][rows])

    take_part(last)
    for t in range(last, 0, -1):
        add_tile(t)
    near[1] = applied(0, last, 0, 2)
    early_code[1] = encode(adjust(last, near[1]))
    send_early(1)
    pl.when(nearby)(start_first)

    @pl.when(both(has_prev, nearby))
    def _():
        first_back(0)

    @pl.when(has_prev)
    def _():
        for piece in range(1, len(cross_spans)):
            first_back(piece)
        early_copy(0).wait_recv()
        place(0, 0, decode(early_got[0]))

    @pl.when(jnp.logical_not(has_prev))
    def _():
        put(0, 0, jnp.zeros((TILE, TILE), F32))
        for sweep in range(SWEEPS):
            place(sweep, 0, jnp.zeros((TILE, limit.shape[1]), F32))

    place(1, 1, finish(0, near[0] + applied(0, 0, 0, 1)))

    @pl.when(has_prev)
    def _():
        for piece, (first, size) in enumerate(back_spans[1]):
            rows = slice(first, first + size)
            back_code[1, rows] = encode_wide(across(1, rows))
            back_copy(1, first, size, 1 + piece // 3).start()

    for t in range(1, last):
        place(1, t + 1, finish(t, applied(0, t, 0, 3)))

    near[0] = applied(1, 0, 1, 2)
    for t in range(1, last - 1):
        out[t * TILE : (t + 1) * TILE] = finish(t, applied(1, t, 0, 3))
    inner = applied(1, last - 1, 0, 2)
    edge = applied(1, last, 0, 1)

    @pl.when(jnp.logical_not(has_next))
    def _():
        back_got[...] = jnp.zeros_like(back_got)

    @pl.when(has_next)
    def _():
        back_copy(0, 0, TILE, 0).wait_recv()

    place(1, tiles, finish(last, near[1] + decode(back_got[0])))
    out[(last - 1) * TILE : last * TILE] = finish(last - 1, inner + applied(1, last - 1, 2, 1))
    edge = edge + applied(1, last, 1, 1)

    @pl.when(has_prev)
    def _():
        early_copy(2).wait_recv()
        early_copy(1).wait_recv()
        scale = keep_of(tail_got[pl.ds(0, 1), :])
        value = decode(early_got[1]) - (1.0 - shrinkage) * (first_term[...] * scale)
        place(1, 0, soften(value, scale))

    out[:TILE] = finish(0, near[0] + applied(1, 0, 0, 1))

    for k in range(len(peers)):
        diag_copy(k).wait_send()

        @pl.when(has_prev)
        def _():
            code_copy(k, 0, total_rows, 0).wait_send()

        @pl.when(jnp.logical_not(has_prev))
        def _():
            code_copy(k, 0, cross_at, 0).wait_send()

    @pl.when(has_next)
    def _():
        geno_sent().wait_send()
        early_sent().wait_send()
        early_copy(2).wait_send()

    for first, size in ((0, 3 * QUARTER), (3 * QUARTER, QUARTER)):
        rows = slice(first, first + size)

        @pl.when(has_next)
        def _():
            back_copy(1, first, size, 1 + first // (3 * QUARTER)).wait_recv()

        combined = edge[rows] + decode_wide(back_got[1, rows])
        out[last * TILE + rows.start : last * TILE + rows.stop] = finish(last, combined, rows)


    @pl.when(has_prev)
    def _():
        back_sent().wait_send()


def local(genotypes, marginal, start_effects, thresholds):
    samples, variants = genotypes.shape
    traits = marginal.shape[1]
    tiles = variants // TILE
    var_size, samp_size = lax.axis_size("var"), lax.axis_size("samp")
    others = samp_size - 1
    rows = tiles * (HALF + TILE)
    dma = pltpu.SemaphoreType.DMA
    body = functools.partial(
        kernel, tiles, var_size, samp_size, 1.0 / (samples * samp_size)
    )
    return pl.pallas_call(
        body,
        out_shape=jax.ShapeDtypeStruct((variants, traits), F32),
        in_specs=[pl.BlockSpec(memory_space=pltpu.HBM)] * 4,
        out_specs=pl.BlockSpec(memory_space=pltpu.VMEM),
        scratch_shapes=[
            pltpu.VMEM((samples, variants), BF16),
            pltpu.VMEM((samples, TILE), BF16),
            pltpu.VMEM((2, variants, traits), F32),
            pltpu.VMEM((1, traits), F32),
            pltpu.VMEM((rows, TILE), F32),
            pltpu.VMEM((rows, TILE), BF16),
            pltpu.VMEM((others, rows, TILE), BF16),
            pltpu.VMEM((8, TILE), F32),
            pltpu.VMEM((others, 8, TILE), F32),
            pltpu.VMEM((tiles, TILE, 3 * TILE), BF16),
            pltpu.VMEM((tiles, TILE, 3 * TILE), BF16),
            pltpu.VMEM((SWEEPS, (tiles + 1) * TILE, traits), BF16),
            pltpu.VMEM((SWEEPS, (tiles + 1) * TILE, traits), BF16),
            pltpu.VMEM((TILE, TILE), BF16),
            pltpu.VMEM((TILE, TILE), BF16),
            pltpu.VMEM((TILE, traits), F32),
            pltpu.VMEM((2, TILE, traits), BF16),
            pltpu.VMEM((2, TILE, traits), BF16),
            pltpu.VMEM((8, TILE), F32),
            pltpu.VMEM((8, TILE), F32),
            pltpu.VMEM((SWEEPS, TILE, traits), BF16),
            pltpu.VMEM((SWEEPS, TILE, traits), BF16),
            pltpu.VMEM((2, TILE, traits), F32),
            dma((4,)),
            dma,
            dma((3,)),
            dma((others, 2)),
            dma((others, 5)),
            dma((2,)),
            dma((3,)),
            dma,
            dma((3,)),
        ],
        compiler_params=pltpu.CompilerParams(
            collective_id=0, has_side_effects=True, vmem_limit_bytes=VMEM_BYTES
        ),
    )(*(
        pltpu.with_memory_space_constraint(array, pltpu.HBM)
        for array in (genotypes, marginal, start_effects, thresholds[None, :])
    ))


def solution(mesh):
    in_specs = (P("samp", "var"), P("var", "samp"), P("var", "samp"), P("samp"))
    out_specs = P("var", "samp")
    return jax.shard_map(local, mesh=mesh, in_specs=in_specs, out_specs=out_specs, check_vma=False)
```

```python
import functools

import jax
import jax.numpy as jnp
from jax import lax
from jax.experimental import pallas as pl
from jax.experimental.pallas import tpu as pltpu
from jax.sharding import PartitionSpec as P

TILE = 256
HALF = TILE // 2
SWEEPS = 2
QUARTER = TILE // 4
RELAYS = 3
TINY = 2.0**-126
VMEM_BYTES = 40 * 1024 * 1024
LD_SCALE = 1024.0

shrinkage = 0.2
MESH = pl.DeviceIdType.MESH
F32 = jnp.float32
BF16 = jnp.bfloat16


def encode(value):
    square = value * value
    fourth = square * square
    eighth = fourth * fourth
    return jnp.where(value < 0, -eighth, eighth).astype(BF16)


def decode(code):
    code = code.astype(F32)
    size = jnp.abs(code)
    fourth_root = lax.rsqrt(lax.rsqrt(jnp.maximum(size, TINY)))
    root = jnp.where(size < TINY, 0.0, fourth_root * lax.rsqrt(fourth_root))
    return jnp.where(code < 0, -root, root)


def encode_wide(value):
    square = value * value
    fourth = square * square
    return jnp.where(value < 0, -fourth, fourth).astype(BF16)


def decode_wide(code):
    code = code.astype(F32)
    size = jnp.abs(code)
    root = jnp.where(size < TINY, 0.0, lax.rsqrt(lax.rsqrt(jnp.maximum(size, TINY))))
    return jnp.where(code < 0, -root, root)


def split(value):
    high = value.astype(BF16)
    return high, (value - high.astype(F32)).astype(BF16)


def iota_pair(size):
    row = lax.broadcasted_iota(jnp.int32, (size, size), 0)
    col = lax.broadcasted_iota(jnp.int32, (size, size), 1)
    return row, col


def pack_symmetric(tile):
    row, col = iota_pair(HALF)
    mixed = jnp.where(row < col, tile[:HALF, :HALF], tile[HALF:, HALF:])
    return jnp.concatenate([mixed, tile[:HALF, HALF:]], axis=1)


def unpack_symmetric(packed):
    row, col = iota_pair(HALF)
    mixed, corner = packed[:, :HALF], packed[:, HALF:]
    upper = jnp.where(row < col, mixed, 0.0)
    lower = jnp.where(row > col, mixed, 0.0)
    first = jnp.concatenate([upper + upper.T, corner], axis=1)
    second = jnp.concatenate([corner.T, lower + lower.T], axis=1)
    return jnp.concatenate([first, second], axis=0)


def gram(left, right):
    return lax.dot_general(left, right, (((0,), (0,)), ((), ())), preferred_element_type=F32)


def kernel(
    tiles, var_size, samp_size, inv_total,
    geno_hbm, marg_hbm, start_hbm, limit_hbm, out,
    geno, halo, table, limit_row, own, code, got, diag, diag_got,
    band_hi, band_lo, eff_hi, eff_lo, cross_hi, cross_lo, first_term,
    early_code, early_got, tail_diag, tail_got, back_code, back_got, near, held,
    load_sem, geno_send, geno_recv, part_send, part_recv,
    early_send, early_recv, back_send, back_recv, held_send, held_recv,
):
    var = lax.axis_index("var")
    samp = lax.axis_index("samp")
    has_prev = var > 0
    has_next = var < var_size - 1
    prev, following = var - 1, var + 1
    nearby = lax.rem(var, 2) == 1
    far = jnp.logical_not(nearby)

    def both(*terms):
        return functools.reduce(jnp.logical_and, terms)

    peers = [lax.rem(samp + k, samp_size) for k in range(1, samp_size)]
    last = tiles - 1
    tail = slice(last * TILE, tiles * TILE)

    step = HALF + TILE
    cross_at = tiles * step - TILE
    total_rows = cross_at + TILE
    halves = range(2)
    cross_spans = [(0, HALF), (HALF, HALF)]
    diag_message = tiles + len(cross_spans)
    marg, start = table.at[0], table.at[1]
    first_cols = pl.ds(0, 2 * TILE)
    other_cols = pl.ds(2 * TILE, (tiles - 2) * TILE)
    loads = [
        pltpu.make_async_copy(geno_hbm.at[:, first_cols], geno.at[:, first_cols], load_sem.at[0]),
        pltpu.make_async_copy(geno_hbm.at[:, other_cols], geno.at[:, other_cols], load_sem.at[1]),
        pltpu.make_async_copy(start_hbm, start, load_sem.at[2]),
        pltpu.make_async_copy(marg_hbm, marg, load_sem.at[2]),
        pltpu.make_async_copy(limit_hbm, limit_row, load_sem.at[3]),
    ]

    barrier = pltpu.get_barrier_semaphore()

    @pl.when(has_prev)
    def _():
        pl.semaphore_signal(barrier, inc=1, device_id={"var": prev}, device_id_type=MESH)

    @pl.when(has_next)
    def _():
        pl.semaphore_signal(barrier, inc=1, device_id={"var": following}, device_id_type=MESH)

    for peer in peers:
        pl.semaphore_signal(barrier, inc=1, device_id={"samp": peer}, device_id_type=MESH)

    routes = [(4 * k + 3, 0, 4 * k + 4, k) for k in range(RELAYS)]
    routes = [route for route in routes if max(route) < var_size]
    waits = has_prev.astype(jnp.int32) + has_next.astype(jnp.int32)
    relayed = var < 0
    for sender, middle, target, _ in routes:
        @pl.when(var == middle)
        def _():
            pl.semaphore_signal(barrier, inc=1, device_id={"var": sender}, device_id_type=MESH)

        @pl.when(var == target)
        def _():
            pl.semaphore_signal(barrier, inc=1, device_id={"var": middle}, device_id_type=MESH)

        waits = waits + (var == sender).astype(jnp.int32) + (var == middle).astype(jnp.int32)
        relayed = jnp.logical_or(relayed, var == sender)

    for copy in loads:
        copy.start()

    pl.semaphore_wait(barrier, len(peers) + waits)

    depth = geno.shape[0]
    cut = depth - depth // 4
    small = depth // 8
    geno_spans = [(0, 0, depth), (1, 0, small), (1, small, cut), (1, cut, depth)]
    piece_rows, piece_cols = pl.ds(0, small), pl.ds(last * TILE + HALF, HALF)

    def outward_copy(middle, slot):
        return pltpu.make_async_remote_copy(
            src_ref=geno_hbm.at[piece_rows, piece_cols], dst_ref=held.at[slot],
            send_sem=geno_send, recv_sem=held_recv.at[slot],
            device_id={"var": middle}, device_id_type=MESH,
        )

    def onward_copy(target, slot):
        return pltpu.make_async_remote_copy(
            src_ref=held.at[slot], dst_ref=halo.at[piece_rows, pl.ds(HALF, HALF)],
            send_sem=held_send.at[slot], recv_sem=geno_recv.at[1],
            device_id={"var": target}, device_id_type=MESH,
        )

    for sender, middle, _, slot in routes:
        @pl.when(var == sender)
        def _():
            outward_copy(middle, slot).start()

    def geno_copy(index):
        half, begin, end = geno_spans[index]
        rows = pl.ds(begin, end - begin)
        return pltpu.make_async_remote_copy(
            src_ref=geno_hbm.at[rows, pl.ds(last * TILE + half * HALF, HALF)],
            dst_ref=halo.at[rows, pl.ds(half * HALF, HALF)],
            send_sem=geno_send, recv_sem=geno_recv.at[index],
            device_id={"var": following}, device_id_type=MESH,
        )

    def geno_sent():
        return pltpu.make_async_remote_copy(
            src_ref=geno_hbm.at[:, pl.ds(last * TILE, TILE)], dst_ref=halo,
            send_sem=geno_send, recv_sem=geno_recv.at[0],
            device_id={"var": following}, device_id_type=MESH,
        )

    @pl.when(has_next)
    def _():
        geno_copy(0).start()

    @pl.when(both(has_next, jnp.logical_not(relayed)))
    def _():
        geno_copy(1).start()

    @pl.when(has_next)
    def _():
        for index in (2, 3):
            geno_copy(index).start()

    def code_copy(k, begin, end, arrival):
        rows = pl.ds(begin, end - begin)
        return pltpu.make_async_remote_copy(
            src_ref=code.at[rows], dst_ref=got.at[k, rows],
            send_sem=part_send.at[k, 0], recv_sem=part_recv.at[k, arrival],
            device_id={"samp": peers[k]}, device_id_type=MESH,
        )

    def diag_copy(k):
        return pltpu.make_async_remote_copy(
            src_ref=diag, dst_ref=diag_got.at[k],
            send_sem=part_send.at[k, 1], recv_sem=part_recv.at[k, 2 + len(cross_spans)],
            device_id={"samp": peers[k]}, device_id_type=MESH,
        )

    def part_copy(k, message):
        if message == diag_message:
            return diag_copy(k)
        if message < tiles:
            begin = message * step
            return code_copy(k, begin, min(begin + step, cross_at), min(message, 1))
        first, size = cross_spans[message - tiles]
        return code_copy(k, cross_at + first, cross_at + first + size, 2 + message - tiles)

    def send_part(message):
        for k in range(len(peers)):
            part_copy(k, message).start()

    def take_part(message):
        for k in range(len(peers)):
            if 0 < message < tiles:
                code_copy(k, step, cross_at, 1).wait_recv()
            else:
                part_copy(k, message).wait_recv()

    diag[...] = jnp.zeros_like(diag)
    row, col = iota_pair(TILE)
    on_diagonal = row == col

    for t in range(tiles):
        if t < 2:
            loads[t].wait()
        reach = min(t + 2, tiles) * TILE
        product = gram(geno[:, t * TILE : (t + 1) * TILE], geno[:, t * TILE : reach])
        product = product * (inv_total * LD_SCALE)
        block = product[:, :TILE]
        diag[pl.ds(t, 1), :] = jnp.sum(jnp.where(on_diagonal, block, 0.0), axis=0, keepdims=True)
        begin = t * step
        packed = pack_symmetric(block)
        own[begin : begin + HALF] = packed
        code[begin : begin + HALF] = encode(packed)
        if t + 1 < tiles:
            beside = product[:, TILE:]
            own[begin + HALF : begin + step] = beside
            code[begin + HALF : begin + step] = encode(beside)
        if t < last:
            pl.when(far if t == 0 else var >= 0)(functools.partial(send_part, t))

    @pl.when(nearby)
    def _():
        for message in (last, diag_message, 0):
            send_part(message)

    pltpu.make_async_copy(table, table, load_sem.at[2]).wait()
    loads[4].wait()

    def place(sweep, slot, value, first=0):
        begin = slot * TILE + first
        high, low = split(value)
        eff_hi[sweep, begin : begin + value.shape[0]] = high
        eff_lo[sweep, begin : begin + value.shape[0]] = low

    early = [(early_code.at[k], early_got.at[k], 0) for k in range(2)] + [(tail_diag, tail_got, 1)]

    def early_copy(k):
        src, dst, departure = early[k]
        return pltpu.make_async_remote_copy(
            src_ref=src, dst_ref=dst, send_sem=early_send.at[departure], recv_sem=early_recv.at[k],
            device_id={"var": following}, device_id_type=MESH,
        )

    def early_sent():
        return pltpu.make_async_remote_copy(
            src_ref=early_code, dst_ref=early_got, send_sem=early_send.at[0], recv_sem=early_recv.at[0],
            device_id={"var": following}, device_id_type=MESH,
        )

    def send_early(k):
        @pl.when(has_next)
        def _():
            early_copy(k).start()

    early_code[0] = encode(start[tail])
    send_early(0)
    for t in range(tiles):
        place(0, t + 1, start[t * TILE : (t + 1) * TILE])

    def summed(begin, size):
        value = own[begin : begin + size]
        for k in range(len(peers)):
            value = value + decode(got[k, begin : begin + size])
        return value

    def put(tile, slot, value, first=0):
        high, low = split(value)
        begin = slot * TILE + first
        band_hi[tile, :, begin : begin + value.shape[1]] = high
        band_lo[tile, :, begin : begin + value.shape[1]] = low

    dot = functools.partial(jnp.dot, preferred_element_type=F32)

    def applied(sweep, tile, first, count):
        across = slice(first * TILE, (first + count) * TILE)
        rows = slice((tile + first) * TILE, (tile + first + count) * TILE)
        high, low = band_hi[tile, :, across], band_lo[tile, :, across]
        near, rest = eff_hi[sweep, rows], eff_lo[sweep, rows]
        return dot(high, near) + (dot(high, rest) + dot(low, near))

    def add_tile(t):
        begin = t * step
        put(t, 1, unpack_symmetric(summed(begin, HALF)) * (1.0 / LD_SCALE))
        if t + 1 < tiles:
            beside = summed(begin + HALF, TILE) * (1.0 / LD_SCALE)
            put(t, 2, beside)
            put(t + 1, 0, beside.T)

    def cross_step(half, now):
        @pl.when(jnp.logical_and(has_prev, now))
        def _():
            begin = cross_at + half * HALF
            for indices in ((0,),) if half == 0 else ((1, 2), (3,)):
                for index in indices:
                    geno_copy(index).wait_recv()
                first, end = geno_spans[indices[0]][1], geno_spans[indices[-1]][2]
                crossing = gram(
                    halo[first:end, half * HALF : (half + 1) * HALF], geno[first:end, :TILE]
                )
                crossing = crossing * (inv_total * LD_SCALE)
                if first > 0:
                    crossing = crossing + own[begin : begin + HALF]
                own[begin : begin + HALF] = crossing
            code[begin : begin + HALF] = encode(crossing)
            for piece, (first, size) in enumerate(cross_spans):
                if first // HALF == half:
                    send_part(tiles + piece)

    for half in halves:
        cross_step(half, nearby)
    for _, middle, target, slot in routes:
        @pl.when(var == middle)
        def _():
            outward_copy(middle, slot).wait_recv()
            onward_copy(target, slot).start()

    def start_first():
        take_part(0)
        add_tile(0)
        near[0] = applied(0, 0, 1, 2)

    cross_step(0, far)

    @pl.when(far)
    def _():
        for message in (last, diag_message):
            send_part(message)
        start_first()

    back_spans = [cross_spans, [(k * QUARTER, QUARTER) for k in range(4)]]

    def back_copy(sweep, first, size, arrival):
        rows = pl.ds(first, size)
        return pltpu.make_async_remote_copy(
            src_ref=back_code.at[sweep, rows], dst_ref=back_got.at[sweep, rows],
            send_sem=back_send, recv_sem=back_recv.at[arrival],
            device_id={"var": prev}, device_id_type=MESH,
        )

    def back_sent():
        return pltpu.make_async_remote_copy(
            src_ref=back_code, dst_ref=back_got, send_sem=back_send, recv_sem=back_recv.at[0],
            device_id={"var": prev}, device_id_type=MESH,
        )

    def across(sweep, rows):
        near, rest = eff_hi[sweep, TILE : 2 * TILE], eff_lo[sweep, TILE : 2 * TILE]
        high, low = cross_hi[rows], cross_lo[rows]
        return dot(high, near) + (dot(high, rest) + dot(low, near))

    def first_back(piece):
        first, size = cross_spans[piece]
        rows = slice(first, first + size)
        take_part(tiles + piece)
        crossing = summed(cross_at + first, size) * (1.0 / LD_SCALE)
        cross_hi[rows], cross_lo[rows] = split(crossing)
        term = across(0, rows)
        first_term[rows] = term
        back_code[0, rows] = encode(term)
        back_copy(0, first, size, 0).start()
        put(0, 0, crossing.T, first)

    cross_step(1, far)

    @pl.when(both(has_prev, far))
    def _():
        first_back(0)

    take_part(diag_message)

    def keep_of(whole):
        column = jnp.sum(jnp.where(on_diagonal, whole, 0.0), axis=1, keepdims=True) * (1.0 / LD_SCALE)
        return 1.0 / ((1.0 - shrinkage) * column + shrinkage)

    keep = []
    for t in range(tiles):
        whole = diag[pl.ds(t, 1), :]
        for k in range(len(peers)):
            whole = whole + diag_got[k, pl.ds(t, 1), :]
        keep.append(keep_of(whole))
        if t == last:
            tail_diag[...] = jnp.broadcast_to(whole, tail_diag.shape)
    send_early(2)
    limit = limit_row[...]

    def adjust(tile, combined, rows=slice(0, TILE)):
        shift = slice(tile * TILE + rows.start, tile * TILE + rows.stop)
        return (marg[shift] - (1.0 - shrinkage) * combined) * keep[tile][rows]

    def soften(value, scale):
        bound = limit * scale
        return value - jnp.clip(value, -bound, bound)

    def finish(tile, combined, rows=slice(0, TILE)):
        return soften(adjust(tile, combined, rows), keep[tile][rows])

    take_part(last)
    for t in range(last, 0, -1):
        add_tile(t)
    near[1] = applied(0, last, 0, 2)
    early_code[1] = encode(adjust(last, near[1]))
    send_early(1)
    pl.when(nearby)(start_first)

    @pl.when(both(has_prev, nearby))
    def _():
        first_back(0)

    @pl.when(has_prev)
    def _():
        for piece in range(1, len(cross_spans)):
            first_back(piece)
        early_copy(0).wait_recv()
        place(0, 0, decode(early_got[0]))

    @pl.when(jnp.logical_not(has_prev))
    def _():
        put(0, 0, jnp.zeros((TILE, TILE), F32))
        for sweep in range(SWEEPS):
            place(sweep, 0, jnp.zeros((TILE, limit.shape[1]), F32))

    place(1, 1, finish(0, near[0] + applied(0, 0, 0, 1)))

    @pl.when(has_prev)
    def _():
        for piece, (first, size) in enumerate(back_spans[1]):
            rows = slice(first, first + size)
            back_code[1, rows] = encode_wide(across(1, rows))
            back_copy(1, first, size, 1 + piece // 3).start()

    for t in range(1, last):
        place(1, t + 1, finish(t, applied(0, t, 0, 3)))

    near[0] = applied(1, 0, 1, 2)
    for t in range(1, last - 1):
        out[t * TILE : (t + 1) * TILE] = finish(t, applied(1, t, 0, 3))
    inner = applied(1, last - 1, 0, 2)
    edge = applied(1, last, 0, 1)

    @pl.when(jnp.logical_not(has_next))
    def _():
        back_got[...] = jnp.zeros_like(back_got)

    @pl.when(has_next)
    def _():
        back_copy(0, 0, TILE, 0).wait_recv()

    place(1, tiles, finish(last, near[1] + decode(back_got[0])))
    out[(last - 1) * TILE : last * TILE] = finish(last - 1, inner + applied(1, last - 1, 2, 1))
    edge = edge + applied(1, last, 1, 1)

    def end_last():
        for first, size in ((0, 3 * QUARTER), (3 * QUARTER, QUARTER)):
            rows = slice(first, first + size)

            @pl.when(has_next)
            def _():
                back_copy(1, first, size, 1 + first // (3 * QUARTER)).wait_recv()

            combined = edge[rows] + decode_wide(back_got[1, rows])
            out[last * TILE + rows.start : last * TILE + rows.stop] = finish(last, combined, rows)

    pl.when(far)(end_last)

    @pl.when(has_prev)
    def _():
        early_copy(2).wait_recv()
        early_copy(1).wait_recv()
        scale = keep_of(tail_got[pl.ds(0, 1), :])
        value = decode(early_got[1]) - (1.0 - shrinkage) * (first_term[...] * scale)
        place(1, 0, soften(value, scale))

    out[:TILE] = finish(0, near[0] + applied(1, 0, 0, 1))

    for k in range(len(peers)):
        diag_copy(k).wait_send()

        @pl.when(has_prev)
        def _():
            code_copy(k, 0, total_rows, 0).wait_send()

        @pl.when(jnp.logical_not(has_prev))
        def _():
            code_copy(k, 0, cross_at, 0).wait_send()

    @pl.when(has_next)
    def _():
        geno_sent().wait_send()
        early_sent().wait_send()
        early_copy(2).wait_send()

    for _, middle, target, slot in routes:
        @pl.when(var == middle)
        def _():
            onward_copy(target, slot).wait_send()

    pl.when(nearby)(end_last)

    @pl.when(has_prev)
    def _():
        back_sent().wait_send()


def local(genotypes, marginal, start_effects, thresholds):
    samples, variants = genotypes.shape
    traits = marginal.shape[1]
    tiles = variants // TILE
    var_size, samp_size = lax.axis_size("var"), lax.axis_size("samp")
    others = samp_size - 1
    rows = tiles * (HALF + TILE)
    dma = pltpu.SemaphoreType.DMA
    body = functools.partial(
        kernel, tiles, var_size, samp_size, 1.0 / (samples * samp_size)
    )
    return pl.pallas_call(
        body,
        out_shape=jax.ShapeDtypeStruct((variants, traits), F32),
        in_specs=[pl.BlockSpec(memory_space=pltpu.HBM)] * 4,
        out_specs=pl.BlockSpec(memory_space=pltpu.VMEM),
        scratch_shapes=[
            pltpu.VMEM((samples, variants), BF16),
            pltpu.VMEM((samples, TILE), BF16),
            pltpu.VMEM((2, variants, traits), F32),
            pltpu.VMEM((1, traits), F32),
            pltpu.VMEM((rows, TILE), F32),
            pltpu.VMEM((rows, TILE), BF16),
            pltpu.VMEM((others, rows, TILE), BF16),
            pltpu.VMEM((8, TILE), F32),
            pltpu.VMEM((others, 8, TILE), F32),
            pltpu.VMEM((tiles, TILE, 3 * TILE), BF16),
            pltpu.VMEM((tiles, TILE, 3 * TILE), BF16),
            pltpu.VMEM((SWEEPS, (tiles + 1) * TILE, traits), BF16),
            pltpu.VMEM((SWEEPS, (tiles + 1) * TILE, traits), BF16),
            pltpu.VMEM((TILE, TILE), BF16),
            pltpu.VMEM((TILE, TILE), BF16),
            pltpu.VMEM((TILE, traits), F32),
            pltpu.VMEM((2, TILE, traits), BF16),
            pltpu.VMEM((2, TILE, traits), BF16),
            pltpu.VMEM((8, TILE), F32),
            pltpu.VMEM((8, TILE), F32),
            pltpu.VMEM((SWEEPS, TILE, traits), BF16),
            pltpu.VMEM((SWEEPS, TILE, traits), BF16),
            pltpu.VMEM((2, TILE, traits), F32),
            pltpu.VMEM((RELAYS, samples // 8, HALF), BF16),
            dma((4,)),
            dma,
            dma((4,)),
            dma((others, 2)),
            dma((others, 5)),
            dma((2,)),
            dma((3,)),
            dma,
            dma((3,)),
            dma((RELAYS,)),
            dma((RELAYS,)),
        ],
        compiler_params=pltpu.CompilerParams(
            collective_id=0, has_side_effects=True, vmem_limit_bytes=VMEM_BYTES
        ),
    )(*(
        pltpu.with_memory_space_constraint(array, pltpu.HBM)
        for array in (genotypes, marginal, start_effects, thresholds[None, :])
    ))


def solution(mesh):
    in_specs = (P("samp", "var"), P("var", "samp"), P("var", "samp"), P("samp"))
    out_specs = P("var", "samp")
    return jax.shard_map(local, mesh=mesh, in_specs=in_specs, out_specs=out_specs, check_vma=False)
```

```python
import functools

import jax
import jax.numpy as jnp
from jax import lax
from jax.experimental import pallas as pl
from jax.experimental.pallas import tpu as pltpu
from jax.sharding import PartitionSpec as P

TILE = 256
HALF = TILE // 2
SWEEPS = 2
QUARTER = TILE // 4
RELAYS = 3
TINY = 2.0**-126
VMEM_BYTES = 40 * 1024 * 1024
LD_SCALE = 1024.0

shrinkage = 0.2
MESH = pl.DeviceIdType.MESH
F32 = jnp.float32
BF16 = jnp.bfloat16


def encode(value):
    square = value * value
    fourth = square * square
    eighth = fourth * fourth
    return jnp.where(value < 0, -eighth, eighth).astype(BF16)


def decode(code):
    code = code.astype(F32)
    size = jnp.abs(code)
    fourth_root = lax.rsqrt(lax.rsqrt(jnp.maximum(size, TINY)))
    root = jnp.where(size < TINY, 0.0, fourth_root * lax.rsqrt(fourth_root))
    return jnp.where(code < 0, -root, root)


def encode_wide(value):
    square = value * value
    fourth = square * square
    return jnp.where(value < 0, -fourth, fourth).astype(BF16)


def decode_wide(code):
    code = code.astype(F32)
    size = jnp.abs(code)
    root = jnp.where(size < TINY, 0.0, lax.rsqrt(lax.rsqrt(jnp.maximum(size, TINY))))
    return jnp.where(code < 0, -root, root)


def split(value):
    high = value.astype(BF16)
    return high, (value - high.astype(F32)).astype(BF16)


def iota_pair(size):
    row = lax.broadcasted_iota(jnp.int32, (size, size), 0)
    col = lax.broadcasted_iota(jnp.int32, (size, size), 1)
    return row, col


def pack_symmetric(tile):
    row, col = iota_pair(HALF)
    mixed = jnp.where(row < col, tile[:HALF, :HALF], tile[HALF:, HALF:])
    return jnp.concatenate([mixed, tile[:HALF, HALF:]], axis=1)


def unpack_symmetric(packed):
    row, col = iota_pair(HALF)
    mixed, corner = packed[:, :HALF], packed[:, HALF:]
    upper = jnp.where(row < col, mixed, 0.0)
    lower = jnp.where(row > col, mixed, 0.0)
    first = jnp.concatenate([upper + upper.T, corner], axis=1)
    second = jnp.concatenate([corner.T, lower + lower.T], axis=1)
    return jnp.concatenate([first, second], axis=0)


def gram(left, right):
    return lax.dot_general(left, right, (((0,), (0,)), ((), ())), preferred_element_type=F32)


def kernel(
    tiles, var_size, samp_size, inv_total,
    geno_hbm, marg_hbm, start_hbm, limit_hbm, out,
    geno, halo, table, limit_row, own, code, got, diag, diag_got,
    band_hi, band_lo, eff_hi, eff_lo, cross_hi, cross_lo, first_term,
    early_code, early_got, tail_diag, tail_got, back_code, back_got, near, held,
    extra_code, extra_got, half_code, half_got,
    load_sem, geno_send, geno_recv, part_send, part_recv,
    early_send, early_recv, back_send, back_recv, held_send, held_recv, extra_send, extra_recv,
):
    var = lax.axis_index("var")
    samp = lax.axis_index("samp")
    has_prev = var > 0
    has_next = var < var_size - 1
    prev, following = var - 1, var + 1
    nearby = lax.rem(var, 2) == 1
    far = jnp.logical_not(nearby)

    leads, follows = jnp.logical_and(var == 1, has_next), var == 2

    def both(*terms):
        return functools.reduce(jnp.logical_and, terms)

    peers = [lax.rem(samp + k, samp_size) for k in range(1, samp_size)]
    last = tiles - 1
    tail = slice(last * TILE, tiles * TILE)

    step = HALF + TILE
    cross_at = tiles * step - TILE
    total_rows = cross_at + TILE
    halves = range(2)
    cross_spans = [(0, HALF), (HALF, HALF)]
    diag_message = tiles + len(cross_spans)
    marg, start = table.at[0], table.at[1]
    first_cols = pl.ds(0, 2 * TILE)
    other_cols = pl.ds(2 * TILE, (tiles - 2) * TILE)
    loads = [
        pltpu.make_async_copy(geno_hbm.at[:, first_cols], geno.at[:, first_cols], load_sem.at[0]),
        pltpu.make_async_copy(geno_hbm.at[:, other_cols], geno.at[:, other_cols], load_sem.at[1]),
        pltpu.make_async_copy(start_hbm, start, load_sem.at[2]),
        pltpu.make_async_copy(marg_hbm, marg, load_sem.at[2]),
        pltpu.make_async_copy(limit_hbm, limit_row, load_sem.at[3]),
    ]

    barrier = pltpu.get_barrier_semaphore()

    @pl.when(has_prev)
    def _():
        pl.semaphore_signal(barrier, inc=1, device_id={"var": prev}, device_id_type=MESH)

    @pl.when(has_next)
    def _():
        pl.semaphore_signal(barrier, inc=1, device_id={"var": following}, device_id_type=MESH)

    for peer in peers:
        pl.semaphore_signal(barrier, inc=1, device_id={"samp": peer}, device_id_type=MESH)

    routes = [(4 * k + 3, 0, 4 * k + 4, k) for k in range(RELAYS)]
    routes = [route for route in routes if max(route) < var_size]
    waits = has_prev.astype(jnp.int32) + has_next.astype(jnp.int32)
    relayed = var < 0
    for sender, middle, target, _ in routes:
        @pl.when(var == middle)
        def _():
            pl.semaphore_signal(barrier, inc=1, device_id={"var": sender}, device_id_type=MESH)

        @pl.when(var == target)
        def _():
            pl.semaphore_signal(barrier, inc=1, device_id={"var": middle}, device_id_type=MESH)

        waits = waits + (var == sender).astype(jnp.int32) + (var == middle).astype(jnp.int32)
        relayed = jnp.logical_or(relayed, var == sender)

    for copy in loads:
        copy.start()

    pl.semaphore_wait(barrier, len(peers) + waits)

    depth = geno.shape[0]
    cut = depth - depth // 4
    small = depth // 8
    geno_spans = [(0, 0, depth), (1, 0, small), (1, small, cut), (1, cut, depth)]
    piece_rows, piece_cols = pl.ds(0, small), pl.ds(last * TILE + HALF, HALF)

    def outward_copy(middle, slot):
        return pltpu.make_async_remote_copy(
            src_ref=geno_hbm.at[piece_rows, piece_cols], dst_ref=held.at[slot],
            send_sem=geno_send, recv_sem=held_recv.at[slot],
            device_id={"var": middle}, device_id_type=MESH,
        )

    def onward_copy(target, slot):
        return pltpu.make_async_remote_copy(
            src_ref=held.at[slot], dst_ref=halo.at[piece_rows, pl.ds(HALF, HALF)],
            send_sem=held_send, recv_sem=geno_recv.at[1],
            device_id={"var": target}, device_id_type=MESH,
        )

    for sender, middle, _, slot in routes:
        @pl.when(var == sender)
        def _():
            outward_copy(middle, slot).start()

    def geno_copy(index):
        half, begin, end = geno_spans[index]
        rows = pl.ds(begin, end - begin)
        return pltpu.make_async_remote_copy(
            src_ref=geno_hbm.at[rows, pl.ds(last * TILE + half * HALF, HALF)],
            dst_ref=halo.at[rows, pl.ds(half * HALF, HALF)],
            send_sem=geno_send, recv_sem=geno_recv.at[index],
            device_id={"var": following}, device_id_type=MESH,
        )

    def geno_sent():
        return pltpu.make_async_remote_copy(
            src_ref=geno_hbm.at[:, pl.ds(last * TILE, TILE)], dst_ref=halo,
            send_sem=geno_send, recv_sem=geno_recv.at[0],
            device_id={"var": following}, device_id_type=MESH,
        )

    @pl.when(has_next)
    def _():
        geno_copy(0).start()

    @pl.when(both(has_next, jnp.logical_not(relayed)))
    def _():
        geno_copy(1).start()

    @pl.when(has_next)
    def _():
        for index in (2, 3):
            geno_copy(index).start()

    def code_copy(k, begin, end, arrival):
        rows = pl.ds(begin, end - begin)
        return pltpu.make_async_remote_copy(
            src_ref=code.at[rows], dst_ref=got.at[k, rows],
            send_sem=part_send.at[k, 0], recv_sem=part_recv.at[k, arrival],
            device_id={"samp": peers[k]}, device_id_type=MESH,
        )

    def diag_copy(k):
        return pltpu.make_async_remote_copy(
            src_ref=diag, dst_ref=diag_got.at[k],
            send_sem=part_send.at[k, 1], recv_sem=part_recv.at[k, 2 + len(cross_spans)],
            device_id={"samp": peers[k]}, device_id_type=MESH,
        )

    def part_copy(k, message):
        if message == diag_message:
            return diag_copy(k)
        if message < tiles:
            begin = message * step
            return code_copy(k, begin, min(begin + step, cross_at), min(message, 1))
        first, size = cross_spans[message - tiles]
        return code_copy(k, cross_at + first, cross_at + first + size, 2 + message - tiles)

    def send_part(message):
        for k in range(len(peers)):
            part_copy(k, message).start()

    def take_part(message):
        for k in range(len(peers)):
            if 0 < message < tiles:
                code_copy(k, step, cross_at, 1).wait_recv()
            else:
                part_copy(k, message).wait_recv()

    diag[...] = jnp.zeros_like(diag)
    row, col = iota_pair(TILE)
    on_diagonal = row == col

    for t in range(tiles):
        if t < 2:
            loads[t].wait()
        reach = min(t + 2, tiles) * TILE
        product = gram(geno[:, t * TILE : (t + 1) * TILE], geno[:, t * TILE : reach])
        product = product * (inv_total * LD_SCALE)
        block = product[:, :TILE]
        diag[pl.ds(t, 1), :] = jnp.sum(jnp.where(on_diagonal, block, 0.0), axis=0, keepdims=True)
        begin = t * step
        packed = pack_symmetric(block)
        own[begin : begin + HALF] = packed
        code[begin : begin + HALF] = encode(packed)
        if t + 1 < tiles:
            beside = product[:, TILE:]
            own[begin + HALF : begin + step] = beside
            code[begin + HALF : begin + step] = encode(beside)
        if t < last:
            pl.when(far if t == 0 else var >= 0)(functools.partial(send_part, t))

    @pl.when(nearby)
    def _():
        for message in (last, diag_message, 0):
            send_part(message)

    pltpu.make_async_copy(table, table, load_sem.at[2]).wait()
    loads[4].wait()

    def place(sweep, slot, value, cols=slice(None)):
        begin = slot * TILE
        high, low = split(value)
        eff_hi[sweep, begin : begin + TILE, cols] = high
        eff_lo[sweep, begin : begin + TILE, cols] = low

    traits = start_hbm.shape[1]
    width = traits // 2 if traits % 256 == 0 else traits
    sides = [slice(begin, begin + width) for begin in range(0, traits, width)]
    full = slice(0, traits)
    early = [(early_code.at[0], early_got.at[0], 0), (tail_diag, tail_got, 1)]
    for side in sides:
        cols = pl.ds(side.start, width)
        early.append((early_code.at[1, :, cols], early_got.at[1, :, cols], 0))

    def early_copy(k):
        src, dst, departure = early[k]
        return pltpu.make_async_remote_copy(
            src_ref=src, dst_ref=dst, send_sem=early_send.at[departure], recv_sem=early_recv.at[k],
            device_id={"var": following}, device_id_type=MESH,
        )

    def early_sent():
        return pltpu.make_async_remote_copy(
            src_ref=early_code, dst_ref=early_got, send_sem=early_send.at[0], recv_sem=early_recv.at[0],
            device_id={"var": following}, device_id_type=MESH,
        )

    def send_early(k):
        @pl.when(has_next)
        def _():
            early_copy(k).start()

    extras = [(extra_code, extra_got), (half_code, half_got)]

    def extra_copy(k):
        src, dst = extras[k]
        return pltpu.make_async_remote_copy(
            src_ref=src, dst_ref=dst, send_sem=extra_send.at[k], recv_sem=extra_recv.at[k],
            device_id={"var": prev}, device_id_type=MESH,
        )

    early_code[0] = encode(start[tail])
    send_early(0)

    @pl.when(follows)
    def _():
        extra_code[...] = encode(start[:TILE])
        extra_copy(0).start()

    for t in range(tiles):
        place(0, t + 1, start[t * TILE : (t + 1) * TILE])

    def summed(begin, size):
        value = own[begin : begin + size]
        for k in range(len(peers)):
            value = value + decode(got[k, begin : begin + size])
        return value

    def put(tile, slot, value, first=0):
        high, low = split(value)
        begin = slot * TILE + first
        band_hi[tile, :, begin : begin + value.shape[1]] = high
        band_lo[tile, :, begin : begin + value.shape[1]] = low

    dot = functools.partial(jnp.dot, preferred_element_type=F32)

    def applied(sweep, tile, first, count, cols=slice(None)):
        across = slice(first * TILE, (first + count) * TILE)
        rows = slice((tile + first) * TILE, (tile + first + count) * TILE)
        high, low = band_hi[tile, :, across], band_lo[tile, :, across]
        near, rest = eff_hi[sweep, rows, cols], eff_lo[sweep, rows, cols]
        return dot(high, near) + (dot(high, rest) + dot(low, near))

    def add_tile(t):
        begin = t * step
        put(t, 1, unpack_symmetric(summed(begin, HALF)) * (1.0 / LD_SCALE))
        if t + 1 < tiles:
            beside = summed(begin + HALF, TILE) * (1.0 / LD_SCALE)
            put(t, 2, beside)
            put(t + 1, 0, beside.T)

    def cross_step(half, now):
        @pl.when(jnp.logical_and(has_prev, now))
        def _():
            begin = cross_at + half * HALF
            for indices in ((0,),) if half == 0 else ((1, 2), (3,)):
                for index in indices:
                    geno_copy(index).wait_recv()
                first, end = geno_spans[indices[0]][1], geno_spans[indices[-1]][2]
                crossing = gram(
                    halo[first:end, half * HALF : (half + 1) * HALF], geno[first:end, :TILE]
                )
                crossing = crossing * (inv_total * LD_SCALE)
                if first > 0:
                    crossing = crossing + own[begin : begin + HALF]
                own[begin : begin + HALF] = crossing
            code[begin : begin + HALF] = encode(crossing)
            for piece, (first, size) in enumerate(cross_spans):
                if first // HALF == half:
                    send_part(tiles + piece)

    for half in halves:
        cross_step(half, nearby)
    for _, middle, target, slot in routes:
        @pl.when(var == middle)
        def _():
            outward_copy(middle, slot).wait_recv()
            onward_copy(target, slot).start()

    def start_first():
        take_part(0)
        add_tile(0)
        near[0] = applied(0, 0, 1, 2)

    cross_step(0, far)

    @pl.when(far)
    def _():
        for message in (last, diag_message):
            send_part(message)
        start_first()

    back_spans = [cross_spans, [(k * QUARTER, QUARTER) for k in range(4)]]

    def back_copy(begin, size, arrival):
        rows = pl.ds(begin, size)
        return pltpu.make_async_remote_copy(
            src_ref=back_code.at[rows], dst_ref=back_got.at[rows],
            send_sem=back_send, recv_sem=back_recv.at[arrival],
            device_id={"var": prev}, device_id_type=MESH,
        )

    def across(sweep, rows):
        near, rest = eff_hi[sweep, TILE : 2 * TILE], eff_lo[sweep, TILE : 2 * TILE]
        high, low = cross_hi[rows], cross_lo[rows]
        return dot(high, near) + (dot(high, rest) + dot(low, near))

    def first_back(piece, product=True):
        first, size = cross_spans[piece]
        rows = slice(first, first + size)
        take_part(tiles + piece)
        scaled = summed(cross_at + first, size)
        if not product:
            half_code[...] = encode(scaled)
            extra_copy(1).start()
        crossing = scaled * (1.0 / LD_SCALE)
        cross_hi[rows], cross_lo[rows] = split(crossing)
        if product:
            term = across(0, rows)
            first_term[rows] = term
            back_code[rows] = encode(term)
            back_copy(first, size, 0).start()
        put(0, 0, crossing.T, first)

    cross_step(1, far)

    @pl.when(both(has_prev, far))
    def _():
        first_back(0)

    take_part(diag_message)

    def keep_of(whole):
        column = jnp.sum(jnp.where(on_diagonal, whole, 0.0), axis=1, keepdims=True) * (1.0 / LD_SCALE)
        return 1.0 / ((1.0 - shrinkage) * column + shrinkage)

    keep = []
    for t in range(tiles):
        whole = diag[pl.ds(t, 1), :]
        for k in range(len(peers)):
            whole = whole + diag_got[k, pl.ds(t, 1), :]
        keep.append(keep_of(whole))
        if t == last:
            tail_diag[...] = jnp.broadcast_to(whole, tail_diag.shape)
    send_early(1)
    limit = limit_row[...]

    every = slice(0, TILE)

    def adjust(tile, combined, rows=every, cols=full):
        shift = slice(tile * TILE + rows.start, tile * TILE + rows.stop)
        return (marg[shift, cols] - (1.0 - shrinkage) * combined) * keep[tile][rows]

    def soften(value, scale, cols=full):
        bound = limit[:, cols] * scale
        return value - jnp.clip(value, -bound, bound)

    def finish(tile, combined, rows=every, cols=full):
        return soften(adjust(tile, combined, rows, cols), keep[tile][rows], cols)

    take_part(last)
    for t in range(last, 0, -1):
        add_tile(t)
    near[1] = applied(0, last, 0, 2)
    for k, side in enumerate(sides):
        early_code[1, :, side] = encode(adjust(last, near[1, :, side], every, side))
        send_early(2 + k)
    pl.when(nearby)(start_first)

    @pl.when(both(has_prev, nearby))
    def _():
        first_back(0)

    @pl.when(both(has_prev, jnp.logical_not(follows)))
    def _():
        first_back(1)

    @pl.when(follows)
    def _():
        first_back(1, False)

    @pl.when(has_prev)
    def _():
        early_copy(0).wait_recv()
        place(0, 0, decode(early_got[0]))

    @pl.when(jnp.logical_not(has_prev))
    def _():
        put(0, 0, jnp.zeros((TILE, TILE), F32))
        for sweep in range(SWEEPS):
            place(sweep, 0, jnp.zeros((TILE, limit.shape[1]), F32))

    place(1, 1, finish(0, near[0] + applied(0, 0, 0, 1)))

    @pl.when(has_prev)
    def _():
        for piece, (first, size) in enumerate(back_spans[1]):
            rows = slice(first, first + size)
            back_code[TILE + first : TILE + first + size] = encode_wide(across(1, rows))
            back_copy(TILE + first, size, 1 + piece // 3).start()

    @pl.when(follows)
    def _():
        first_term[HALF:] = across(0, slice(HALF, TILE))

    for t in range(1, last):
        place(1, t + 1, finish(t, applied(0, t, 0, 3)))

    near[0] = applied(1, 0, 1, 2)
    for t in range(1, last - 1):
        out[t * TILE : (t + 1) * TILE] = finish(t, applied(1, t, 0, 3))
    inner = applied(1, last - 1, 0, 2)
    edge = applied(1, last, 0, 1)

    @pl.when(jnp.logical_not(has_next))
    def _():
        back_got[...] = jnp.zeros_like(back_got)

    @pl.when(leads)
    def _():
        extra_copy(0).wait_recv()
        effects_hi, effects_lo = split(decode(extra_got[...]))
        back_copy(0, HALF, 0).wait_recv()
        back_got[HALF:TILE] = jnp.zeros((TILE - HALF, limit.shape[1]), BF16)
        extra_copy(1).wait_recv()
        high, low = split(decode(half_got[...]) * (1.0 / LD_SCALE))
        term = dot(high, effects_hi) + (dot(high, effects_lo) + dot(low, effects_hi))
        near[1, HALF:TILE] = near[1, HALF:TILE] + term

    @pl.when(both(has_next, jnp.logical_not(leads)))
    def _():
        back_copy(0, TILE, 0).wait_recv()

    place(1, tiles, finish(last, near[1] + decode(back_got[:TILE])))
    out[(last - 1) * TILE : last * TILE] = finish(last - 1, inner + applied(1, last - 1, 2, 1))
    edge = edge + applied(1, last, 1, 1)

    def end_last():
        for first, size in ((0, 3 * QUARTER), (3 * QUARTER, QUARTER)):
            rows = slice(first, first + size)

            @pl.when(has_next)
            def _():
                back_copy(TILE + first, size, 1 + first // (3 * QUARTER)).wait_recv()

            combined = edge[rows] + decode_wide(back_got[TILE + first : TILE + first + size])
            out[last * TILE + rows.start : last * TILE + rows.stop] = finish(last, combined, rows)

    pl.when(far)(end_last)

    @pl.when(has_prev)
    def _():
        early_copy(1).wait_recv()

    for k, side in enumerate(sides):
        @pl.when(has_prev)
        def _():
            early_copy(2 + k).wait_recv()
            scale = keep_of(tail_got[pl.ds(0, 1), :])
            value = decode(early_got[1, :, side])
            value = value - (1.0 - shrinkage) * (first_term[:, side] * scale)
            place(1, 0, soften(value, scale, side), side)

        combined = near[0, :, side] + applied(1, 0, 0, 1, side)
        out[:TILE, side] = finish(0, combined, every, side)

    for k in range(len(peers)):
        diag_copy(k).wait_send()

        @pl.when(has_prev)
        def _():
            code_copy(k, 0, total_rows, 0).wait_send()

        @pl.when(jnp.logical_not(has_prev))
        def _():
            code_copy(k, 0, cross_at, 0).wait_send()

    @pl.when(has_next)
    def _():
        geno_sent().wait_send()
        early_sent().wait_send()
        early_copy(1).wait_send()

    if routes:
        @pl.when(var == 0)
        def _():
            pltpu.make_async_remote_copy(
                src_ref=held.at[pl.ds(0, len(routes))], dst_ref=held.at[pl.ds(0, len(routes))],
                send_sem=held_send, recv_sem=geno_recv.at[1],
                device_id={"var": following}, device_id_type=MESH,
            ).wait_send()

    pl.when(nearby)(end_last)

    @pl.when(both(has_prev, jnp.logical_not(follows)))
    def _():
        back_copy(0, 2 * TILE, 0).wait_send()

    @pl.when(follows)
    def _():
        back_copy(0, TILE + HALF, 0).wait_send()
        for k in range(len(extras)):
            extra_copy(k).wait_send()


def local(genotypes, marginal, start_effects, thresholds):
    samples, variants = genotypes.shape
    traits = marginal.shape[1]
    tiles = variants // TILE
    var_size, samp_size = lax.axis_size("var"), lax.axis_size("samp")
    others = samp_size - 1
    rows = tiles * (HALF + TILE)
    dma = pltpu.SemaphoreType.DMA
    body = functools.partial(
        kernel, tiles, var_size, samp_size, 1.0 / (samples * samp_size)
    )
    return pl.pallas_call(
        body,
        out_shape=jax.ShapeDtypeStruct((variants, traits), F32),
        in_specs=[pl.BlockSpec(memory_space=pltpu.HBM)] * 4,
        out_specs=pl.BlockSpec(memory_space=pltpu.VMEM),
        scratch_shapes=[
            pltpu.VMEM((samples, variants), BF16),
            pltpu.VMEM((samples, TILE), BF16),
            pltpu.VMEM((2, variants, traits), F32),
            pltpu.VMEM((1, traits), F32),
            pltpu.VMEM((rows, TILE), F32),
            pltpu.VMEM((rows, TILE), BF16),
            pltpu.VMEM((others, rows, TILE), BF16),
            pltpu.VMEM((8, TILE), F32),
            pltpu.VMEM((others, 8, TILE), F32),
            pltpu.VMEM((tiles, TILE, 3 * TILE), BF16),
            pltpu.VMEM((tiles, TILE, 3 * TILE), BF16),
            pltpu.VMEM((SWEEPS, (tiles + 1) * TILE, traits), BF16),
            pltpu.VMEM((SWEEPS, (tiles + 1) * TILE, traits), BF16),
            pltpu.VMEM((TILE, TILE), BF16),
            pltpu.VMEM((TILE, TILE), BF16),
            pltpu.VMEM((TILE, traits), F32),
            pltpu.VMEM((2, TILE, traits), BF16),
            pltpu.VMEM((2, TILE, traits), BF16),
            pltpu.VMEM((8, TILE), F32),
            pltpu.VMEM((8, TILE), F32),
            pltpu.VMEM((SWEEPS * TILE, traits), BF16),
            pltpu.VMEM((SWEEPS * TILE, traits), BF16),
            pltpu.VMEM((2, TILE, traits), F32),
            pltpu.VMEM((RELAYS, samples // 8, HALF), BF16),
            pltpu.VMEM((TILE, traits), BF16),
            pltpu.VMEM((TILE, traits), BF16),
            pltpu.VMEM((HALF, TILE), BF16),
            pltpu.VMEM((HALF, TILE), BF16),
            dma((4,)),
            dma,
            dma((4,)),
            dma((others, 2)),
            dma((others, 5)),
            dma((2,)),
            dma((4,)),
            dma,
            dma((3,)),
            dma,
            dma((RELAYS,)),
            dma((2,)),
            dma((2,)),
        ],
        compiler_params=pltpu.CompilerParams(
            collective_id=0, has_side_effects=True, vmem_limit_bytes=VMEM_BYTES
        ),
    )(*(
        pltpu.with_memory_space_constraint(array, pltpu.HBM)
        for array in (genotypes, marginal, start_effects, thresholds[None, :])
    ))


def solution(mesh):
    in_specs = (P("samp", "var"), P("var", "samp"), P("var", "samp"), P("samp"))
    out_specs = P("var", "samp")
    return jax.shard_map(local, mesh=mesh, in_specs=in_specs, out_specs=out_specs, check_vma=False)
```

```python
import functools

import jax
import jax.numpy as jnp
from jax import lax
from jax.experimental import pallas as pl
from jax.experimental.pallas import tpu as pltpu
from jax.sharding import PartitionSpec as P

TILE = 256
HALF = TILE // 2
SWEEPS = 2
QUARTER = TILE // 4
RELAYS = 3
TINY = 2.0**-126
VMEM_BYTES = 40 * 1024 * 1024
LD_SCALE = 1024.0

shrinkage = 0.2
MESH = pl.DeviceIdType.MESH
F32 = jnp.float32
BF16 = jnp.bfloat16


def encode(value):
    square = value * value
    fourth = square * square
    eighth = fourth * fourth
    return jnp.where(value < 0, -eighth, eighth).astype(BF16)


def decode(code):
    code = code.astype(F32)
    size = jnp.abs(code)
    fourth_root = lax.rsqrt(lax.rsqrt(jnp.maximum(size, TINY)))
    root = jnp.where(size < TINY, 0.0, fourth_root * lax.rsqrt(fourth_root))
    return jnp.where(code < 0, -root, root)


def encode_wide(value):
    square = value * value
    fourth = square * square
    return jnp.where(value < 0, -fourth, fourth).astype(BF16)


def decode_wide(code):
    code = code.astype(F32)
    size = jnp.abs(code)
    root = jnp.where(size < TINY, 0.0, lax.rsqrt(lax.rsqrt(jnp.maximum(size, TINY))))
    return jnp.where(code < 0, -root, root)


def split(value):
    high = value.astype(BF16)
    return high, (value - high.astype(F32)).astype(BF16)


def iota_pair(size):
    row = lax.broadcasted_iota(jnp.int32, (size, size), 0)
    col = lax.broadcasted_iota(jnp.int32, (size, size), 1)
    return row, col


def pack_symmetric(tile):
    row, col = iota_pair(HALF)
    mixed = jnp.where(row < col, tile[:HALF, :HALF], tile[HALF:, HALF:])
    return jnp.concatenate([mixed, tile[:HALF, HALF:]], axis=1)


def unpack_symmetric(packed):
    row, col = iota_pair(HALF)
    mixed, corner = packed[:, :HALF], packed[:, HALF:]
    upper = jnp.where(row < col, mixed, 0.0)
    lower = jnp.where(row > col, mixed, 0.0)
    first = jnp.concatenate([upper + upper.T, corner], axis=1)
    second = jnp.concatenate([corner.T, lower + lower.T], axis=1)
    return jnp.concatenate([first, second], axis=0)


def gram(left, right):
    return lax.dot_general(left, right, (((0,), (0,)), ((), ())), preferred_element_type=F32)


def kernel(
    tiles, var_size, samp_size, inv_total,
    geno_hbm, marg_hbm, start_hbm, limit_hbm, out,
    geno, halo, table, limit_row, own, code, got, diag, diag_got,
    band_hi, band_lo, eff_hi, eff_lo, cross_hi, cross_lo, first_term,
    early_code, early_got, tail_diag, tail_got, back_code, back_got, near, held,
    extra_code, extra_got, half_code, half_got,
    load_sem, geno_send, geno_recv, part_send, part_recv,
    early_send, early_recv, back_send, back_recv, held_send, held_recv, extra_send, extra_recv,
):
    var = lax.axis_index("var")
    samp = lax.axis_index("samp")
    has_prev = var > 0
    has_next = var < var_size - 1
    prev, following = var - 1, var + 1
    nearby = lax.rem(var, 2) == 1
    far = jnp.logical_not(nearby)

    leads, follows = jnp.logical_and(var == 1, has_next), var == 2

    def both(*terms):
        return functools.reduce(jnp.logical_and, terms)

    peers = [lax.rem(samp + k, samp_size) for k in range(1, samp_size)]
    last = tiles - 1
    tail = slice(last * TILE, tiles * TILE)

    step = HALF + TILE
    cross_at = tiles * step - TILE
    total_rows = cross_at + TILE
    halves = range(2)
    cross_spans = [(0, HALF), (HALF, HALF)]
    diag_message = tiles + len(cross_spans)
    marg, start = table.at[0], table.at[1]
    first_cols = pl.ds(0, 2 * TILE)
    other_cols = pl.ds(2 * TILE, (tiles - 2) * TILE)
    loads = [
        pltpu.make_async_copy(geno_hbm.at[:, first_cols], geno.at[:, first_cols], load_sem.at[0]),
        pltpu.make_async_copy(geno_hbm.at[:, other_cols], geno.at[:, other_cols], load_sem.at[1]),
        pltpu.make_async_copy(start_hbm, start, load_sem.at[2]),
        pltpu.make_async_copy(marg_hbm, marg, load_sem.at[2]),
        pltpu.make_async_copy(limit_hbm, limit_row, load_sem.at[3]),
    ]

    barrier = pltpu.get_barrier_semaphore()

    @pl.when(has_prev)
    def _():
        pl.semaphore_signal(barrier, inc=1, device_id={"var": prev}, device_id_type=MESH)

    @pl.when(has_next)
    def _():
        pl.semaphore_signal(barrier, inc=1, device_id={"var": following}, device_id_type=MESH)

    for peer in peers:
        pl.semaphore_signal(barrier, inc=1, device_id={"samp": peer}, device_id_type=MESH)

    routes = [(4 * k + 3, 0, 4 * k + 4, k) for k in range(RELAYS)]
    routes = [route for route in routes if max(route) < var_size]
    waits = has_prev.astype(jnp.int32) + has_next.astype(jnp.int32)
    relayed = var < 0
    for sender, middle, target, _ in routes:
        @pl.when(var == middle)
        def _():
            pl.semaphore_signal(barrier, inc=1, device_id={"var": sender}, device_id_type=MESH)

        @pl.when(var == target)
        def _():
            pl.semaphore_signal(barrier, inc=1, device_id={"var": middle}, device_id_type=MESH)

        waits = waits + (var == sender).astype(jnp.int32) + (var == middle).astype(jnp.int32)
        relayed = jnp.logical_or(relayed, var == sender)

    for copy in loads:
        copy.start()

    pl.semaphore_wait(barrier, len(peers) + waits)

    depth = geno.shape[0]
    cut = depth - depth // 4
    small = depth // 8
    geno_spans = [(0, 0, depth), (1, 0, small), (1, small, cut), (1, cut, depth)]
    piece_rows, piece_cols = pl.ds(0, small), pl.ds(last * TILE + HALF, HALF)

    def outward_copy(middle, slot):
        return pltpu.make_async_remote_copy(
            src_ref=geno_hbm.at[piece_rows, piece_cols], dst_ref=held.at[slot],
            send_sem=geno_send, recv_sem=held_recv.at[slot],
            device_id={"var": middle}, device_id_type=MESH,
        )

    def onward_copy(target, slot):
        return pltpu.make_async_remote_copy(
            src_ref=held.at[slot], dst_ref=halo.at[piece_rows, pl.ds(HALF, HALF)],
            send_sem=held_send, recv_sem=geno_recv.at[1],
            device_id={"var": target}, device_id_type=MESH,
        )

    for sender, middle, _, slot in routes:
        @pl.when(var == sender)
        def _():
            outward_copy(middle, slot).start()

    def geno_copy(index):
        half, begin, end = geno_spans[index]
        rows = pl.ds(begin, end - begin)
        return pltpu.make_async_remote_copy(
            src_ref=geno_hbm.at[rows, pl.ds(last * TILE + half * HALF, HALF)],
            dst_ref=halo.at[rows, pl.ds(half * HALF, HALF)],
            send_sem=geno_send, recv_sem=geno_recv.at[index],
            device_id={"var": following}, device_id_type=MESH,
        )

    def geno_sent():
        return pltpu.make_async_remote_copy(
            src_ref=geno_hbm.at[:, pl.ds(last * TILE, TILE)], dst_ref=halo,
            send_sem=geno_send, recv_sem=geno_recv.at[0],
            device_id={"var": following}, device_id_type=MESH,
        )

    @pl.when(has_next)
    def _():
        geno_copy(0).start()

    @pl.when(both(has_next, jnp.logical_not(relayed)))
    def _():
        geno_copy(1).start()

    @pl.when(has_next)
    def _():
        for index in (2, 3):
            geno_copy(index).start()

    def code_copy(k, begin, end, arrival):
        rows = pl.ds(begin, end - begin)
        return pltpu.make_async_remote_copy(
            src_ref=code.at[rows], dst_ref=got.at[k, rows],
            send_sem=part_send.at[k, 0], recv_sem=part_recv.at[k, arrival],
            device_id={"samp": peers[k]}, device_id_type=MESH,
        )

    def diag_copy(k):
        return pltpu.make_async_remote_copy(
            src_ref=diag, dst_ref=diag_got.at[k],
            send_sem=part_send.at[k, 1], recv_sem=part_recv.at[k, 2 + len(cross_spans)],
            device_id={"samp": peers[k]}, device_id_type=MESH,
        )

    def part_copy(k, message):
        if message == diag_message:
            return diag_copy(k)
        if message < tiles:
            begin = message * step
            return code_copy(k, begin, min(begin + step, cross_at), min(message, 1))
        first, size = cross_spans[message - tiles]
        return code_copy(k, cross_at + first, cross_at + first + size, 2 + message - tiles)

    def send_part(message):
        for k in range(len(peers)):
            part_copy(k, message).start()

    def take_part(message):
        for k in range(len(peers)):
            if 0 < message < tiles:
                code_copy(k, step, cross_at, 1).wait_recv()
            else:
                part_copy(k, message).wait_recv()

    diag[...] = jnp.zeros_like(diag)
    row, col = iota_pair(TILE)
    on_diagonal = row == col

    for t in range(tiles):
        if t < 2:
            loads[t].wait()
        reach = min(t + 2, tiles) * TILE
        product = gram(geno[:, t * TILE : (t + 1) * TILE], geno[:, t * TILE : reach])
        product = product * (inv_total * LD_SCALE)
        block = product[:, :TILE]
        diag[pl.ds(t, 1), :] = jnp.sum(jnp.where(on_diagonal, block, 0.0), axis=0, keepdims=True)
        begin = t * step
        packed = pack_symmetric(block)
        own[begin : begin + HALF] = packed
        code[begin : begin + HALF] = encode(packed)
        if t + 1 < tiles:
            beside = product[:, TILE:]
            own[begin + HALF : begin + step] = beside
            code[begin + HALF : begin + step] = encode(beside)
        if t < last:
            pl.when(far if t == 0 else var >= 0)(functools.partial(send_part, t))

    @pl.when(nearby)
    def _():
        for message in (last, diag_message, 0):
            send_part(message)

    pltpu.make_async_copy(table, table, load_sem.at[2]).wait()
    loads[4].wait()

    def place(sweep, slot, value, cols=slice(None)):
        begin = slot * TILE
        high, low = split(value)
        eff_hi[sweep, begin : begin + TILE, cols] = high
        eff_lo[sweep, begin : begin + TILE, cols] = low

    traits = start_hbm.shape[1]
    turn = max(traits // 512 * 384, traits % 512)
    sides = [slice(begin, end) for begin, end in ((0, turn), (turn, traits)) if begin < end]
    full = slice(0, traits)
    early = [(early_code.at[0], early_got.at[0], 0), (tail_diag, tail_got, 1)]
    for side in sides:
        cols = pl.ds(side.start, side.stop - side.start)
        early.append((early_code.at[1, :, cols], early_got.at[1, :, cols], 0))

    def early_copy(k):
        src, dst, departure = early[k]
        return pltpu.make_async_remote_copy(
            src_ref=src, dst_ref=dst, send_sem=early_send.at[departure], recv_sem=early_recv.at[k],
            device_id={"var": following}, device_id_type=MESH,
        )

    def early_sent():
        return pltpu.make_async_remote_copy(
            src_ref=early_code, dst_ref=early_got, send_sem=early_send.at[0], recv_sem=early_recv.at[0],
            device_id={"var": following}, device_id_type=MESH,
        )

    def send_early(k):
        @pl.when(has_next)
        def _():
            early_copy(k).start()

    extras = [(extra_code, extra_got), (half_code, half_got)]

    def extra_copy(k):
        src, dst = extras[k]
        return pltpu.make_async_remote_copy(
            src_ref=src, dst_ref=dst, send_sem=extra_send.at[k], recv_sem=extra_recv.at[k],
            device_id={"var": prev}, device_id_type=MESH,
        )

    early_code[0] = encode(start[tail])
    send_early(0)

    @pl.when(follows)
    def _():
        extra_code[...] = encode(start[:TILE])
        extra_copy(0).start()

    for t in range(tiles):
        place(0, t + 1, start[t * TILE : (t + 1) * TILE])

    def summed(begin, size):
        value = own[begin : begin + size]
        for k in range(len(peers)):
            value = value + decode(got[k, begin : begin + size])
        return value

    def put(tile, slot, value, first=0):
        high, low = split(value)
        begin = slot * TILE + first
        band_hi[tile, :, begin : begin + value.shape[1]] = high
        band_lo[tile, :, begin : begin + value.shape[1]] = low

    dot = functools.partial(jnp.dot, preferred_element_type=F32)

    def applied(sweep, tile, first, count, cols=slice(None)):
        across = slice(first * TILE, (first + count) * TILE)
        rows = slice((tile + first) * TILE, (tile + first + count) * TILE)
        high, low = band_hi[tile, :, across], band_lo[tile, :, across]
        near, rest = eff_hi[sweep, rows, cols], eff_lo[sweep, rows, cols]
        return dot(high, near) + (dot(high, rest) + dot(low, near))

    def add_tile(t):
        begin = t * step
        put(t, 1, unpack_symmetric(summed(begin, HALF)) * (1.0 / LD_SCALE))
        if t + 1 < tiles:
            beside = summed(begin + HALF, TILE) * (1.0 / LD_SCALE)
            put(t, 2, beside)
            put(t + 1, 0, beside.T)

    def cross_step(half, now):
        @pl.when(jnp.logical_and(has_prev, now))
        def _():
            begin = cross_at + half * HALF
            for indices in ((0,),) if half == 0 else ((1, 2), (3,)):
                for index in indices:
                    geno_copy(index).wait_recv()
                first, end = geno_spans[indices[0]][1], geno_spans[indices[-1]][2]
                crossing = gram(
                    halo[first:end, half * HALF : (half + 1) * HALF], geno[first:end, :TILE]
                )
                crossing = crossing * (inv_total * LD_SCALE)
                if first > 0:
                    crossing = crossing + own[begin : begin + HALF]
                own[begin : begin + HALF] = crossing
            code[begin : begin + HALF] = encode(crossing)
            for piece, (first, size) in enumerate(cross_spans):
                if first // HALF == half:
                    send_part(tiles + piece)

    for half in halves:
        cross_step(half, nearby)
    for _, middle, target, slot in routes:
        @pl.when(var == middle)
        def _():
            outward_copy(middle, slot).wait_recv()
            onward_copy(target, slot).start()

    def start_first():
        take_part(0)
        add_tile(0)
        near[0] = applied(0, 0, 1, 2)

    cross_step(0, far)

    @pl.when(far)
    def _():
        for message in (last, diag_message):
            send_part(message)
        start_first()

    back_spans = [cross_spans, [(k * QUARTER, QUARTER) for k in range(4)]]

    def back_copy(begin, size, arrival):
        rows = pl.ds(begin, size)
        return pltpu.make_async_remote_copy(
            src_ref=back_code.at[rows], dst_ref=back_got.at[rows],
            send_sem=back_send, recv_sem=back_recv.at[arrival],
            device_id={"var": prev}, device_id_type=MESH,
        )

    def across(sweep, rows):
        near, rest = eff_hi[sweep, TILE : 2 * TILE], eff_lo[sweep, TILE : 2 * TILE]
        high, low = cross_hi[rows], cross_lo[rows]
        return dot(high, near) + (dot(high, rest) + dot(low, near))

    def first_back(piece, product=True):
        first, size = cross_spans[piece]
        rows = slice(first, first + size)
        take_part(tiles + piece)
        scaled = summed(cross_at + first, size)
        if not product:
            half_code[...] = encode(scaled)
            extra_copy(1).start()
        crossing = scaled * (1.0 / LD_SCALE)
        cross_hi[rows], cross_lo[rows] = split(crossing)
        if product:
            term = across(0, rows)
            first_term[rows] = term
            back_code[rows] = encode(term)
            back_copy(first, size, 0).start()
        put(0, 0, crossing.T, first)

    cross_step(1, far)

    @pl.when(both(has_prev, far))
    def _():
        first_back(0)

    take_part(diag_message)

    def keep_of(whole):
        column = jnp.sum(jnp.where(on_diagonal, whole, 0.0), axis=1, keepdims=True) * (1.0 / LD_SCALE)
        return 1.0 / ((1.0 - shrinkage) * column + shrinkage)

    keep = []
    for t in range(tiles):
        whole = diag[pl.ds(t, 1), :]
        for k in range(len(peers)):
            whole = whole + diag_got[k, pl.ds(t, 1), :]
        keep.append(keep_of(whole))
        if t == last:
            tail_diag[...] = jnp.broadcast_to(whole, tail_diag.shape)
    send_early(1)
    limit = limit_row[...]

    every = slice(0, TILE)

    def adjust(tile, combined, rows=every, cols=full):
        shift = slice(tile * TILE + rows.start, tile * TILE + rows.stop)
        return (marg[shift, cols] - (1.0 - shrinkage) * combined) * keep[tile][rows]

    def soften(value, scale, cols=full):
        bound = limit[:, cols] * scale
        return value - jnp.clip(value, -bound, bound)

    def finish(tile, combined, rows=every, cols=full):
        return soften(adjust(tile, combined, rows, cols), keep[tile][rows], cols)

    take_part(last)
    for t in range(last, 0, -1):
        add_tile(t)
    near[1] = applied(0, last, 0, 2)
    for k, side in enumerate(sides):
        early_code[1, :, side] = encode(adjust(last, near[1, :, side], every, side))
        send_early(2 + k)
    pl.when(nearby)(start_first)

    @pl.when(both(has_prev, nearby))
    def _():
        first_back(0)

    @pl.when(both(has_prev, jnp.logical_not(follows)))
    def _():
        first_back(1)

    def take_start():
        early_copy(0).wait_recv()
        place(0, 0, decode(early_got[0]))

    @pl.when(follows)
    def _():
        take_start()
        first_back(1, False)

    pl.when(both(has_prev, jnp.logical_not(follows)))(take_start)

    @pl.when(jnp.logical_not(has_prev))
    def _():
        put(0, 0, jnp.zeros((TILE, TILE), F32))
        for sweep in range(SWEEPS):
            place(sweep, 0, jnp.zeros((TILE, limit.shape[1]), F32))

    place(1, 1, finish(0, near[0] + applied(0, 0, 0, 1)))

    @pl.when(has_prev)
    def _():
        for piece, (first, size) in enumerate(back_spans[1]):
            rows = slice(first, first + size)
            back_code[TILE + first : TILE + first + size] = encode_wide(across(1, rows))
            back_copy(TILE + first, size, 1 + piece // 3).start()

    @pl.when(follows)
    def _():
        first_term[HALF:] = across(0, slice(HALF, TILE))

    for t in range(1, last):
        place(1, t + 1, finish(t, applied(0, t, 0, 3)))

    near[0] = applied(1, 0, 1, 2)
    for t in range(1, last - 1):
        out[t * TILE : (t + 1) * TILE] = finish(t, applied(1, t, 0, 3))
    inner = applied(1, last - 1, 0, 2)
    edge = applied(1, last, 0, 1)

    @pl.when(jnp.logical_not(has_next))
    def _():
        back_got[...] = jnp.zeros_like(back_got)

    @pl.when(leads)
    def _():
        extra_copy(0).wait_recv()
        effects_hi, effects_lo = split(decode(extra_got[...]))
        back_copy(0, HALF, 0).wait_recv()
        back_got[HALF:TILE] = jnp.zeros((TILE - HALF, limit.shape[1]), BF16)
        extra_copy(1).wait_recv()
        high, low = split(decode(half_got[...]) * (1.0 / LD_SCALE))
        term = dot(high, effects_hi) + (dot(high, effects_lo) + dot(low, effects_hi))
        near[1, HALF:TILE] = near[1, HALF:TILE] + term

    @pl.when(both(has_next, jnp.logical_not(leads)))
    def _():
        back_copy(0, TILE, 0).wait_recv()

    place(1, tiles, finish(last, near[1] + decode(back_got[:TILE])))
    out[(last - 1) * TILE : last * TILE] = finish(last - 1, inner + applied(1, last - 1, 2, 1))
    edge = edge + applied(1, last, 1, 1)

    def end_last():
        for first, size in ((0, 3 * QUARTER), (3 * QUARTER, QUARTER)):
            rows = slice(first, first + size)

            @pl.when(has_next)
            def _():
                back_copy(TILE + first, size, 1 + first // (3 * QUARTER)).wait_recv()

            combined = edge[rows] + decode_wide(back_got[TILE + first : TILE + first + size])
            out[last * TILE + rows.start : last * TILE + rows.stop] = finish(last, combined, rows)

    pl.when(far)(end_last)

    @pl.when(has_prev)
    def _():
        early_copy(1).wait_recv()

    for k, side in enumerate(sides):
        @pl.when(has_prev)
        def _():
            early_copy(2 + k).wait_recv()
            scale = keep_of(tail_got[pl.ds(0, 1), :])
            value = decode(early_got[1, :, side])
            value = value - (1.0 - shrinkage) * (first_term[:, side] * scale)
            place(1, 0, soften(value, scale, side), side)

        combined = near[0, :, side] + applied(1, 0, 0, 1, side)
        out[:TILE, side] = finish(0, combined, every, side)

    for k in range(len(peers)):
        diag_copy(k).wait_send()

        @pl.when(has_prev)
        def _():
            code_copy(k, 0, total_rows, 0).wait_send()

        @pl.when(jnp.logical_not(has_prev))
        def _():
            code_copy(k, 0, cross_at, 0).wait_send()

    @pl.when(has_next)
    def _():
        geno_sent().wait_send()
        early_sent().wait_send()
        early_copy(1).wait_send()

    if routes:
        @pl.when(var == 0)
        def _():
            pltpu.make_async_remote_copy(
                src_ref=held.at[pl.ds(0, len(routes))], dst_ref=held.at[pl.ds(0, len(routes))],
                send_sem=held_send, recv_sem=geno_recv.at[1],
                device_id={"var": following}, device_id_type=MESH,
            ).wait_send()

    pl.when(nearby)(end_last)

    @pl.when(both(has_prev, jnp.logical_not(follows)))
    def _():
        back_copy(0, 2 * TILE, 0).wait_send()

    @pl.when(follows)
    def _():
        back_copy(0, TILE + HALF, 0).wait_send()
        for k in range(len(extras)):
            extra_copy(k).wait_send()


def local(genotypes, marginal, start_effects, thresholds):
    samples, variants = genotypes.shape
    traits = marginal.shape[1]
    tiles = variants // TILE
    var_size, samp_size = lax.axis_size("var"), lax.axis_size("samp")
    others = samp_size - 1
    rows = tiles * (HALF + TILE)
    dma = pltpu.SemaphoreType.DMA
    body = functools.partial(
        kernel, tiles, var_size, samp_size, 1.0 / (samples * samp_size)
    )
    return pl.pallas_call(
        body,
        out_shape=jax.ShapeDtypeStruct((variants, traits), F32),
        in_specs=[pl.BlockSpec(memory_space=pltpu.HBM)] * 4,
        out_specs=pl.BlockSpec(memory_space=pltpu.VMEM),
        scratch_shapes=[
            pltpu.VMEM((samples, variants), BF16),
            pltpu.VMEM((samples, TILE), BF16),
            pltpu.VMEM((2, variants, traits), F32),
            pltpu.VMEM((1, traits), F32),
            pltpu.VMEM((rows, TILE), F32),
            pltpu.VMEM((rows, TILE), BF16),
            pltpu.VMEM((others, rows, TILE), BF16),
            pltpu.VMEM((8, TILE), F32),
            pltpu.VMEM((others, 8, TILE), F32),
            pltpu.VMEM((tiles, TILE, 3 * TILE), BF16),
            pltpu.VMEM((tiles, TILE, 3 * TILE), BF16),
            pltpu.VMEM((SWEEPS, (tiles + 1) * TILE, traits), BF16),
            pltpu.VMEM((SWEEPS, (tiles + 1) * TILE, traits), BF16),
            pltpu.VMEM((TILE, TILE), BF16),
            pltpu.VMEM((TILE, TILE), BF16),
            pltpu.VMEM((TILE, traits), F32),
            pltpu.VMEM((2, TILE, traits), BF16),
            pltpu.VMEM((2, TILE, traits), BF16),
            pltpu.VMEM((8, TILE), F32),
            pltpu.VMEM((8, TILE), F32),
            pltpu.VMEM((SWEEPS * TILE, traits), BF16),
            pltpu.VMEM((SWEEPS * TILE, traits), BF16),
            pltpu.VMEM((2, TILE, traits), F32),
            pltpu.VMEM((RELAYS, samples // 8, HALF), BF16),
            pltpu.VMEM((TILE, traits), BF16),
            pltpu.VMEM((TILE, traits), BF16),
            pltpu.VMEM((HALF, TILE), BF16),
            pltpu.VMEM((HALF, TILE), BF16),
            dma((4,)),
            dma,
            dma((4,)),
            dma((others, 2)),
            dma((others, 5)),
            dma((2,)),
            dma((4,)),
            dma,
            dma((3,)),
            dma,
            dma((RELAYS,)),
            dma((2,)),
            dma((2,)),
        ],
        compiler_params=pltpu.CompilerParams(
            collective_id=0, has_side_effects=True, vmem_limit_bytes=VMEM_BYTES
        ),
    )(*(
        pltpu.with_memory_space_constraint(array, pltpu.HBM)
        for array in (genotypes, marginal, start_effects, thresholds[None, :])
    ))


def solution(mesh):
    in_specs = (P("samp", "var"), P("var", "samp"), P("var", "samp"), P("samp"))
    out_specs = P("var", "samp")
    return jax.shard_map(local, mesh=mesh, in_specs=in_specs, out_specs=out_specs, check_vma=False)
```

```python
import functools

import jax
import jax.numpy as jnp
from jax import lax
from jax.experimental import pallas as pl
from jax.experimental.pallas import tpu as pltpu
from jax.sharding import PartitionSpec as P

TILE = 256
HALF = TILE // 2
SWEEPS = 2
QUARTER = TILE // 4
RELAYS = 3
TINY = 2.0**-126
VMEM_BYTES = 40 * 1024 * 1024
LD_SCALE = 1024.0

shrinkage = 0.2
MESH = pl.DeviceIdType.MESH
F32 = jnp.float32
BF16 = jnp.bfloat16


def encode(value):
    square = value * value
    fourth = square * square
    eighth = fourth * fourth
    return jnp.where(value < 0, -eighth, eighth).astype(BF16)


def decode(code):
    code = code.astype(F32)
    size = jnp.abs(code)
    fourth_root = lax.rsqrt(lax.rsqrt(jnp.maximum(size, TINY)))
    root = jnp.where(size < TINY, 0.0, fourth_root * lax.rsqrt(fourth_root))
    return jnp.where(code < 0, -root, root)


def encode_wide(value):
    square = value * value
    fourth = square * square
    return jnp.where(value < 0, -fourth, fourth).astype(BF16)


def decode_wide(code):
    code = code.astype(F32)
    size = jnp.abs(code)
    root = jnp.where(size < TINY, 0.0, lax.rsqrt(lax.rsqrt(jnp.maximum(size, TINY))))
    return jnp.where(code < 0, -root, root)


def split(value):
    high = value.astype(BF16)
    return high, (value - high.astype(F32)).astype(BF16)


def iota_pair(size):
    row = lax.broadcasted_iota(jnp.int32, (size, size), 0)
    col = lax.broadcasted_iota(jnp.int32, (size, size), 1)
    return row, col


def pack_symmetric(tile):
    row, col = iota_pair(HALF)
    mixed = jnp.where(row < col, tile[:HALF, :HALF], tile[HALF:, HALF:])
    return jnp.concatenate([mixed, tile[:HALF, HALF:]], axis=1)


def unpack_symmetric(packed):
    row, col = iota_pair(HALF)
    mixed, corner = packed[:, :HALF], packed[:, HALF:]
    upper = jnp.where(row < col, mixed, 0.0)
    lower = jnp.where(row > col, mixed, 0.0)
    first = jnp.concatenate([upper + upper.T, corner], axis=1)
    second = jnp.concatenate([corner.T, lower + lower.T], axis=1)
    return jnp.concatenate([first, second], axis=0)


def gram(left, right):
    return lax.dot_general(left, right, (((0,), (0,)), ((), ())), preferred_element_type=F32)


def kernel(
    tiles, var_size, samp_size, inv_total,
    geno_hbm, marg_hbm, start_hbm, limit_hbm, out,
    geno, halo, table, limit_row, own, code, got, diag, diag_got,
    band_hi, band_lo, eff_hi, eff_lo, cross_hi, cross_lo, first_term,
    early_code, early_got, tail_diag, tail_got, back_code, back_got, near, held,
    extra_code, extra_got, half_code, half_got,
    load_sem, geno_send, geno_recv, part_send, part_recv,
    early_send, early_recv, back_send, back_recv, held_send, held_recv, extra_send, extra_recv,
):
    var = lax.axis_index("var")
    samp = lax.axis_index("samp")
    has_prev = var > 0
    has_next = var < var_size - 1
    prev, following = var - 1, var + 1
    nearby = lax.rem(var, 2) == 1
    far = jnp.logical_not(nearby)

    leads, follows = jnp.logical_and(var == 1, has_next), var == 2

    def both(*terms):
        return functools.reduce(jnp.logical_and, terms)

    peers = [lax.rem(samp + k, samp_size) for k in range(1, samp_size)]
    last = tiles - 1
    tail = slice(last * TILE, tiles * TILE)

    step = HALF + TILE
    cross_at = tiles * step - TILE
    total_rows = cross_at + TILE
    halves = range(2)
    cross_spans = [(0, HALF), (HALF, HALF)]
    diag_message = tiles + len(cross_spans)
    marg, start = table.at[0], table.at[1]
    first_cols = pl.ds(0, 2 * TILE)
    other_cols = pl.ds(2 * TILE, (tiles - 2) * TILE)
    loads = [
        pltpu.make_async_copy(geno_hbm.at[:, first_cols], geno.at[:, first_cols], load_sem.at[0]),
        pltpu.make_async_copy(geno_hbm.at[:, other_cols], geno.at[:, other_cols], load_sem.at[1]),
        pltpu.make_async_copy(start_hbm, start, load_sem.at[2]),
        pltpu.make_async_copy(marg_hbm, marg, load_sem.at[2]),
        pltpu.make_async_copy(limit_hbm, limit_row, load_sem.at[3]),
    ]

    barrier = pltpu.get_barrier_semaphore()

    @pl.when(has_prev)
    def _():
        pl.semaphore_signal(barrier, inc=1, device_id={"var": prev}, device_id_type=MESH)

    @pl.when(has_next)
    def _():
        pl.semaphore_signal(barrier, inc=1, device_id={"var": following}, device_id_type=MESH)

    for peer in peers:
        pl.semaphore_signal(barrier, inc=1, device_id={"samp": peer}, device_id_type=MESH)

    routes = [(4 * k + 3, 0, 4 * k + 4, k) for k in range(RELAYS)]
    routes = [route for route in routes if max(route) < var_size]
    waits = has_prev.astype(jnp.int32) + has_next.astype(jnp.int32)
    relayed = var < 0
    for sender, middle, target, _ in routes:
        @pl.when(var == middle)
        def _():
            pl.semaphore_signal(barrier, inc=1, device_id={"var": sender}, device_id_type=MESH)

        @pl.when(var == target)
        def _():
            pl.semaphore_signal(barrier, inc=1, device_id={"var": middle}, device_id_type=MESH)

        waits = waits + (var == sender).astype(jnp.int32) + (var == middle).astype(jnp.int32)
        relayed = jnp.logical_or(relayed, var == sender)

    for copy in loads:
        copy.start()

    pl.semaphore_wait(barrier, len(peers) + waits)

    depth = geno.shape[0]
    cut = depth - depth // 4
    small = depth // 8
    geno_spans = [(0, 0, depth), (1, 0, small), (1, small, cut), (1, cut, depth)]
    arrivals = (0, 1, 1, 2)
    piece_rows, piece_cols = pl.ds(0, small), pl.ds(last * TILE + HALF, HALF)

    def outward_copy(middle, slot):
        return pltpu.make_async_remote_copy(
            src_ref=geno_hbm.at[piece_rows, piece_cols], dst_ref=held.at[slot],
            send_sem=geno_send, recv_sem=held_recv,
            device_id={"var": middle}, device_id_type=MESH,
        )

    def onward_copy(target, slot):
        return pltpu.make_async_remote_copy(
            src_ref=held.at[slot], dst_ref=halo.at[piece_rows, pl.ds(HALF, HALF)],
            send_sem=held_send, recv_sem=geno_recv.at[1],
            device_id={"var": target}, device_id_type=MESH,
        )

    for sender, middle, _, slot in routes:
        @pl.when(var == sender)
        def _():
            outward_copy(middle, slot).start()

    def geno_copy(index):
        half, begin, end = geno_spans[index]
        rows = pl.ds(begin, end - begin)
        return pltpu.make_async_remote_copy(
            src_ref=geno_hbm.at[rows, pl.ds(last * TILE + half * HALF, HALF)],
            dst_ref=halo.at[rows, pl.ds(half * HALF, HALF)],
            send_sem=geno_send, recv_sem=geno_recv.at[arrivals[index]],
            device_id={"var": following}, device_id_type=MESH,
        )

    def geno_taken(half, begin, end, arrival):
        rows, cols = pl.ds(begin, end - begin), pl.ds(half * HALF, HALF)
        pltpu.make_async_remote_copy(
            src_ref=halo.at[rows, cols], dst_ref=halo.at[rows, cols],
            send_sem=geno_send, recv_sem=geno_recv.at[arrival],
            device_id={"var": following}, device_id_type=MESH,
        ).wait_recv()

    def geno_sent():
        return pltpu.make_async_remote_copy(
            src_ref=geno_hbm.at[:, pl.ds(last * TILE, TILE)], dst_ref=halo,
            send_sem=geno_send, recv_sem=geno_recv.at[0],
            device_id={"var": following}, device_id_type=MESH,
        )

    @pl.when(has_next)
    def _():
        geno_copy(0).start()

    @pl.when(both(has_next, jnp.logical_not(relayed)))
    def _():
        geno_copy(1).start()

    @pl.when(has_next)
    def _():
        for index in (2, 3):
            geno_copy(index).start()

    def code_copy(k, begin, end, arrival):
        rows = pl.ds(begin, end - begin)
        return pltpu.make_async_remote_copy(
            src_ref=code.at[rows], dst_ref=got.at[k, rows],
            send_sem=part_send.at[k, 0], recv_sem=part_recv.at[k, arrival],
            device_id={"samp": peers[k]}, device_id_type=MESH,
        )

    def diag_copy(k):
        return pltpu.make_async_remote_copy(
            src_ref=diag, dst_ref=diag_got.at[k],
            send_sem=part_send.at[k, 1], recv_sem=part_recv.at[k, 2 + len(cross_spans)],
            device_id={"samp": peers[k]}, device_id_type=MESH,
        )

    def part_copy(k, message):
        if message == diag_message:
            return diag_copy(k)
        if message < tiles:
            begin = message * step
            return code_copy(k, begin, min(begin + step, cross_at), min(message, 1))
        first, size = cross_spans[message - tiles]
        return code_copy(k, cross_at + first, cross_at + first + size, 2 + message - tiles)

    def send_part(message):
        for k in range(len(peers)):
            part_copy(k, message).start()

    def take_part(message):
        for k in range(len(peers)):
            if 0 < message < tiles:
                code_copy(k, step, cross_at, 1).wait_recv()
            else:
                part_copy(k, message).wait_recv()

    diag[...] = jnp.zeros_like(diag)
    row, col = iota_pair(TILE)
    on_diagonal = row == col

    for t in range(tiles):
        if t < 2:
            loads[t].wait()
        reach = min(t + 2, tiles) * TILE
        product = gram(geno[:, t * TILE : (t + 1) * TILE], geno[:, t * TILE : reach])
        product = product * (inv_total * LD_SCALE)
        block = product[:, :TILE]
        diag[pl.ds(t, 1), :] = jnp.sum(jnp.where(on_diagonal, block, 0.0), axis=0, keepdims=True)
        begin = t * step
        packed = pack_symmetric(block)
        own[begin : begin + HALF] = packed
        code[begin : begin + HALF] = encode(packed)
        if t + 1 < tiles:
            beside = product[:, TILE:]
            own[begin + HALF : begin + step] = beside
            code[begin + HALF : begin + step] = encode(beside)
        if t < last:
            pl.when(far if t == 0 else var >= 0)(functools.partial(send_part, t))

    @pl.when(nearby)
    def _():
        for message in (last, diag_message, 0):
            send_part(message)

    pltpu.make_async_copy(table, table, load_sem.at[2]).wait()
    loads[4].wait()

    def place(sweep, slot, value, cols=slice(None)):
        begin = slot * TILE
        high, low = split(value)
        eff_hi[sweep, begin : begin + TILE, cols] = high
        eff_lo[sweep, begin : begin + TILE, cols] = low

    traits = start_hbm.shape[1]
    turn = max(traits // 512 * 384, traits % 512)
    sides = [slice(begin, end) for begin, end in ((0, turn), (turn, traits)) if begin < end]
    full = slice(0, traits)
    early = [(early_code.at[0], early_got.at[0], 0), (tail_diag, tail_got, 1)]
    for side in sides:
        cols = pl.ds(side.start, side.stop - side.start)
        early.append((early_code.at[1, :, cols], early_got.at[1, :, cols], 0))

    def early_copy(k):
        src, dst, departure = early[k]
        return pltpu.make_async_remote_copy(
            src_ref=src, dst_ref=dst, send_sem=early_send.at[departure], recv_sem=early_recv.at[k],
            device_id={"var": following}, device_id_type=MESH,
        )

    def early_sent():
        return pltpu.make_async_remote_copy(
            src_ref=early_code, dst_ref=early_got, send_sem=early_send.at[0], recv_sem=early_recv.at[0],
            device_id={"var": following}, device_id_type=MESH,
        )

    def send_early(k):
        @pl.when(has_next)
        def _():
            early_copy(k).start()

    extras = [(extra_code, extra_got), (half_code, half_got)]

    def extra_copy(k):
        src, dst = extras[k]
        return pltpu.make_async_remote_copy(
            src_ref=src, dst_ref=dst, send_sem=extra_send, recv_sem=extra_recv.at[k],
            device_id={"var": prev}, device_id_type=MESH,
        )

    early_code[0] = encode(start[tail])
    send_early(0)

    @pl.when(follows)
    def _():
        extra_code[...] = encode(start[:TILE])
        extra_copy(0).start()

    for t in range(tiles):
        place(0, t + 1, start[t * TILE : (t + 1) * TILE])

    def summed(begin, size):
        value = own[begin : begin + size]
        for k in range(len(peers)):
            value = value + decode(got[k, begin : begin + size])
        return value

    def put(tile, slot, value, first=0):
        high, low = split(value)
        begin = slot * TILE + first
        band_hi[tile, :, begin : begin + value.shape[1]] = high
        band_lo[tile, :, begin : begin + value.shape[1]] = low

    dot = functools.partial(jnp.dot, preferred_element_type=F32)

    def applied(sweep, tile, first, count, cols=slice(None)):
        across = slice(first * TILE, (first + count) * TILE)
        rows = slice((tile + first) * TILE, (tile + first + count) * TILE)
        high, low = band_hi[tile, :, across], band_lo[tile, :, across]
        near, rest = eff_hi[sweep, rows, cols], eff_lo[sweep, rows, cols]
        return dot(high, near) + (dot(high, rest) + dot(low, near))

    def add_tile(t):
        begin = t * step
        put(t, 1, unpack_symmetric(summed(begin, HALF)) * (1.0 / LD_SCALE))
        if t + 1 < tiles:
            beside = summed(begin + HALF, TILE) * (1.0 / LD_SCALE)
            put(t, 2, beside)
            put(t + 1, 0, beside.T)

    def cross_step(half, now):
        @pl.when(jnp.logical_and(has_prev, now))
        def _():
            begin = cross_at + half * HALF
            for indices in ((0,),) if half == 0 else ((1, 2), (3,)):
                first, end = geno_spans[indices[0]][1], geno_spans[indices[-1]][2]
                geno_taken(half, first, end, arrivals[indices[0]])
                crossing = gram(
                    halo[first:end, half * HALF : (half + 1) * HALF], geno[first:end, :TILE]
                )
                crossing = crossing * (inv_total * LD_SCALE)
                if first > 0:
                    crossing = crossing + own[begin : begin + HALF]
                own[begin : begin + HALF] = crossing
            code[begin : begin + HALF] = encode(crossing)
            for piece, (first, size) in enumerate(cross_spans):
                if first // HALF == half:
                    send_part(tiles + piece)

    for half in halves:
        cross_step(half, nearby)
    if routes:
        every_slot = held.at[pl.ds(0, len(routes))]

        @pl.when(var == 0)
        def _():
            pltpu.make_async_remote_copy(
                src_ref=every_slot, dst_ref=every_slot, send_sem=held_send, recv_sem=held_recv,
                device_id={"var": following}, device_id_type=MESH,
            ).wait_recv()
            for _, _, target, slot in routes:
                onward_copy(target, slot).start()

    def start_first():
        take_part(0)
        add_tile(0)
        near[0] = applied(0, 0, 1, 2)

    cross_step(0, far)

    @pl.when(far)
    def _():
        for message in (last, diag_message):
            send_part(message)
        start_first()

    back_spans = [cross_spans, [(k * QUARTER, QUARTER) for k in range(4)]]

    def back_copy(begin, size, arrival):
        rows = pl.ds(begin, size)
        return pltpu.make_async_remote_copy(
            src_ref=back_code.at[rows], dst_ref=back_got.at[rows],
            send_sem=back_send, recv_sem=back_recv.at[arrival],
            device_id={"var": prev}, device_id_type=MESH,
        )

    def across(sweep, rows):
        near, rest = eff_hi[sweep, TILE : 2 * TILE], eff_lo[sweep, TILE : 2 * TILE]
        high, low = cross_hi[rows], cross_lo[rows]
        return dot(high, near) + (dot(high, rest) + dot(low, near))

    def first_back(piece, product=True):
        first, size = cross_spans[piece]
        rows = slice(first, first + size)
        take_part(tiles + piece)
        scaled = summed(cross_at + first, size)
        if not product:
            half_code[...] = encode(scaled)
            extra_copy(1).start()
        crossing = scaled * (1.0 / LD_SCALE)
        cross_hi[rows], cross_lo[rows] = split(crossing)
        if product:
            term = across(0, rows)
            first_term[rows] = term
            back_code[rows] = encode(term)
            back_copy(first, size, 0).start()
        put(0, 0, crossing.T, first)

    cross_step(1, far)

    @pl.when(both(has_prev, far))
    def _():
        first_back(0)

    take_part(diag_message)

    def keep_of(whole):
        column = jnp.sum(jnp.where(on_diagonal, whole, 0.0), axis=1, keepdims=True) * (1.0 / LD_SCALE)
        return 1.0 / ((1.0 - shrinkage) * column + shrinkage)

    keep = []
    for t in range(tiles):
        whole = diag[pl.ds(t, 1), :]
        for k in range(len(peers)):
            whole = whole + diag_got[k, pl.ds(t, 1), :]
        keep.append(keep_of(whole))
        if t == last:
            tail_diag[...] = jnp.broadcast_to(whole, tail_diag.shape)
    send_early(1)
    limit = limit_row[...]

    every = slice(0, TILE)

    def adjust(tile, combined, rows=every, cols=full):
        shift = slice(tile * TILE + rows.start, tile * TILE + rows.stop)
        return (marg[shift, cols] - (1.0 - shrinkage) * combined) * keep[tile][rows]

    def soften(value, scale, cols=full):
        bound = limit[:, cols] * scale
        return value - jnp.clip(value, -bound, bound)

    def finish(tile, combined, rows=every, cols=full):
        return soften(adjust(tile, combined, rows, cols), keep[tile][rows], cols)

    take_part(last)
    for t in range(last, 0, -1):
        add_tile(t)
    near[1] = applied(0, last, 0, 2)
    for k, side in enumerate(sides):
        early_code[1, :, side] = encode(adjust(last, near[1, :, side], every, side))
        send_early(2 + k)
    pl.when(nearby)(start_first)

    @pl.when(both(has_prev, nearby))
    def _():
        first_back(0)

    @pl.when(both(has_prev, jnp.logical_not(follows)))
    def _():
        first_back(1)

    def take_start():
        early_copy(0).wait_recv()
        place(0, 0, decode(early_got[0]))

    @pl.when(follows)
    def _():
        take_start()
        first_back(1, False)

    pl.when(both(has_prev, jnp.logical_not(follows)))(take_start)

    @pl.when(jnp.logical_not(has_prev))
    def _():
        put(0, 0, jnp.zeros((TILE, TILE), F32))
        for sweep in range(SWEEPS):
            place(sweep, 0, jnp.zeros((TILE, limit.shape[1]), F32))

    place(1, 1, finish(0, near[0] + applied(0, 0, 0, 1)))

    @pl.when(has_prev)
    def _():
        for piece, (first, size) in enumerate(back_spans[1]):
            rows = slice(first, first + size)
            back_code[TILE + first : TILE + first + size] = encode_wide(across(1, rows))
            back_copy(TILE + first, size, 1 + piece // 3).start()

    @pl.when(follows)
    def _():
        first_term[HALF:] = across(0, slice(HALF, TILE))

    for t in range(1, last):
        place(1, t + 1, finish(t, applied(0, t, 0, 3)))

    near[0] = applied(1, 0, 1, 2)
    for t in range(1, last - 1):
        out[t * TILE : (t + 1) * TILE] = finish(t, applied(1, t, 0, 3))
    inner = applied(1, last - 1, 0, 2)
    edge = applied(1, last, 0, 1)

    @pl.when(jnp.logical_not(has_next))
    def _():
        back_got[...] = jnp.zeros_like(back_got)

    @pl.when(leads)
    def _():
        extra_copy(0).wait_recv()
        effects_hi, effects_lo = split(decode(extra_got[...]))
        back_copy(0, HALF, 0).wait_recv()
        back_got[HALF:TILE] = jnp.zeros((TILE - HALF, limit.shape[1]), BF16)
        extra_copy(1).wait_recv()
        high, low = split(decode(half_got[...]) * (1.0 / LD_SCALE))
        term = dot(high, effects_hi) + (dot(high, effects_lo) + dot(low, effects_hi))
        near[1, HALF:TILE] = near[1, HALF:TILE] + term

    @pl.when(both(has_next, jnp.logical_not(leads)))
    def _():
        back_copy(0, TILE, 0).wait_recv()

    place(1, tiles, finish(last, near[1] + decode(back_got[:TILE])))
    out[(last - 1) * TILE : last * TILE] = finish(last - 1, inner + applied(1, last - 1, 2, 1))
    edge = edge + applied(1, last, 1, 1)

    def end_last():
        for first, size in ((0, 3 * QUARTER), (3 * QUARTER, QUARTER)):
            rows = slice(first, first + size)

            @pl.when(has_next)
            def _():
                back_copy(TILE + first, size, 1 + first // (3 * QUARTER)).wait_recv()

            combined = edge[rows] + decode_wide(back_got[TILE + first : TILE + first + size])
            out[last * TILE + rows.start : last * TILE + rows.stop] = finish(last, combined, rows)

    pl.when(far)(end_last)

    @pl.when(has_prev)
    def _():
        early_copy(1).wait_recv()

    for k, side in enumerate(sides):
        @pl.when(has_prev)
        def _():
            early_copy(2 + k).wait_recv()
            scale = keep_of(tail_got[pl.ds(0, 1), :])
            value = decode(early_got[1, :, side])
            value = value - (1.0 - shrinkage) * (first_term[:, side] * scale)
            place(1, 0, soften(value, scale, side), side)

        combined = near[0, :, side] + applied(1, 0, 0, 1, side)
        out[:TILE, side] = finish(0, combined, every, side)

    for k in range(len(peers)):
        diag_copy(k).wait_send()

        @pl.when(has_prev)
        def _():
            code_copy(k, 0, total_rows, 0).wait_send()

        @pl.when(jnp.logical_not(has_prev))
        def _():
            code_copy(k, 0, cross_at, 0).wait_send()

    @pl.when(has_next)
    def _():
        geno_sent().wait_send()
        early_sent().wait_send()
        early_copy(1).wait_send()

    if routes:
        @pl.when(var == 0)
        def _():
            pltpu.make_async_remote_copy(
                src_ref=held.at[pl.ds(0, len(routes))], dst_ref=held.at[pl.ds(0, len(routes))],
                send_sem=held_send, recv_sem=geno_recv.at[1],
                device_id={"var": following}, device_id_type=MESH,
            ).wait_send()

    pl.when(nearby)(end_last)

    @pl.when(both(has_prev, jnp.logical_not(follows)))
    def _():
        back_copy(0, 2 * TILE, 0).wait_send()

    @pl.when(follows)
    def _():
        back_copy(0, TILE + HALF, 0).wait_send()
        rows = pl.ds(0, TILE + HALF * TILE // extra_code.shape[1])
        pltpu.make_async_remote_copy(
            src_ref=back_code.at[rows], dst_ref=back_got.at[rows],
            send_sem=extra_send, recv_sem=extra_recv.at[0],
            device_id={"var": prev}, device_id_type=MESH,
        ).wait_send()


def local(genotypes, marginal, start_effects, thresholds):
    samples, variants = genotypes.shape
    traits = marginal.shape[1]
    tiles = variants // TILE
    var_size, samp_size = lax.axis_size("var"), lax.axis_size("samp")
    others = samp_size - 1
    rows = tiles * (HALF + TILE)
    dma = pltpu.SemaphoreType.DMA
    body = functools.partial(
        kernel, tiles, var_size, samp_size, 1.0 / (samples * samp_size)
    )
    return pl.pallas_call(
        body,
        out_shape=jax.ShapeDtypeStruct((variants, traits), F32),
        in_specs=[pl.BlockSpec(memory_space=pltpu.HBM)] * 4,
        out_specs=pl.BlockSpec(memory_space=pltpu.VMEM),
        scratch_shapes=[
            pltpu.VMEM((samples, variants), BF16),
            pltpu.VMEM((samples, TILE), BF16),
            pltpu.VMEM((2, variants, traits), F32),
            pltpu.VMEM((1, traits), F32),
            pltpu.VMEM((rows, TILE), F32),
            pltpu.VMEM((rows, TILE), BF16),
            pltpu.VMEM((others, rows, TILE), BF16),
            pltpu.VMEM((8, TILE), F32),
            pltpu.VMEM((others, 8, TILE), F32),
            pltpu.VMEM((tiles, TILE, 3 * TILE), BF16),
            pltpu.VMEM((tiles, TILE, 3 * TILE), BF16),
            pltpu.VMEM((SWEEPS, (tiles + 1) * TILE, traits), BF16),
            pltpu.VMEM((SWEEPS, (tiles + 1) * TILE, traits), BF16),
            pltpu.VMEM((TILE, TILE), BF16),
            pltpu.VMEM((TILE, TILE), BF16),
            pltpu.VMEM((TILE, traits), F32),
            pltpu.VMEM((2, TILE, traits), BF16),
            pltpu.VMEM((2, TILE, traits), BF16),
            pltpu.VMEM((8, TILE), F32),
            pltpu.VMEM((8, TILE), F32),
            pltpu.VMEM((SWEEPS * TILE, traits), BF16),
            pltpu.VMEM((SWEEPS * TILE, traits), BF16),
            pltpu.VMEM((2, TILE, traits), F32),
            pltpu.VMEM((RELAYS, samples // 8, HALF), BF16),
            pltpu.VMEM((TILE, traits), BF16),
            pltpu.VMEM((TILE, traits), BF16),
            pltpu.VMEM((HALF, TILE), BF16),
            pltpu.VMEM((HALF, TILE), BF16),
            dma((4,)),
            dma,
            dma((3,)),
            dma((others, 2)),
            dma((others, 5)),
            dma((2,)),
            dma((4,)),
            dma,
            dma((3,)),
            dma,
            dma,
            dma,
            dma((2,)),
        ],
        compiler_params=pltpu.CompilerParams(
            collective_id=0, has_side_effects=True, vmem_limit_bytes=VMEM_BYTES
        ),
    )(*(
        pltpu.with_memory_space_constraint(array, pltpu.HBM)
        for array in (genotypes, marginal, start_effects, thresholds[None, :])
    ))


def solution(mesh):
    in_specs = (P("samp", "var"), P("var", "samp"), P("var", "samp"), P("samp"))
    out_specs = P("var", "samp")
    return jax.shard_map(local, mesh=mesh, in_specs=in_specs, out_specs=out_specs, check_vma=False)
```
